32 devices in a mesh: grp: 1, seq: 32 (over z, y, x, core).
Axes of the slice: x: 2, y: 2, z: 4, core: 2. Of those that a mesh axis runs over, the one named last changes fastest.
Arguments:
- features: bfloat16 [8192, 768], P(('grp', 'seq')), may hold values from -6 to 6
- targets: int32 [8192, 896], P(('grp', 'seq')), may hold values from 0 to 3
- mappable: int32 [8192], P(('grp', 'seq')), may hold values 0 or 1
- w_in: bfloat16 [2, 768, 384], replicated, may hold values from -0.21875 to 0.21875
- w_conv: bfloat16 [2, 3, 384, 384], replicated, may hold values from -0.1875 to 0.1875
- w_out: bfloat16 [2, 384, 768], replicated, may hold values from -0.3125 to 0.3125
- w_head: bfloat16 [768, 896], replicated, may hold values from -0.109375 to 0.109375
Outputs:
- grad_in: float32 [2, 768, 384], P('grp', 'seq')
- grad_conv: float32 [2, 3, 384, 384], P('grp', None, 'seq')
- grad_out: float32 [2, 384, 768], P('grp', 'seq')
The draws below stay inside these ranges and needn't reach their ends.
All inputs are finite; a program needn't handle non-finite values. No bound on the sum of `mappable` on one device may be relied on, other than what follows from the above.
Results may differ from the reference program's by a relative error of at most 0.0075.
Values may be sent and summed in bfloat16 or wider, within the bound.
A program may use at most 128 MiB of HBM per device.

```python
import math
import jax
import jax.numpy as jnp

D = 768
B = 384
TRACKS = 896
FIRST_DILATION = 2048
SECOND_DILATION = 4096
LEN = 8192


def set_ends(result, rng, least, largest):
    shape = result.shape
    index_at = [jax.random.randint(jax.random.fold_in(rng, axis), (), 0, shape[axis]) for axis in range(len(shape))]
    result = result.at[tuple(index_at)].set(least)
    longest = shape.index(max(shape))
    index_at[longest] = (index_at[longest] + 1) % shape[longest]
    return result.at[tuple(index_at)].set(largest)


def strengthened(drawn, own_key, source, target, parts, factor):
    owner, partner = [(jnp.arange(drawn.shape[dim]) // (drawn.shape[dim] // parts)).reshape([-1 if axis == dim else 1 for axis in range(drawn.ndim)]) for dim in (source, target)]
    chosen = jax.random.permutation(own_key, parts)[partner]
    strong = (owner == chosen) | (owner == (partner + parts // 2) % parts)
    return jnp.where(strong, factor * drawn, drawn)


def steps_of(own_key, extent, shards, low, top_value):
    loudness = 1.0
    for dim, shards_of in shards:
        heights = jax.random.uniform(jax.random.fold_in(jax.random.fold_in(own_key, 6), dim), (shards_of,), jnp.float32, low / len(shards), top_value / len(shards))
        loudness = loudness * jnp.repeat(jnp.exp(heights), extent[dim] // shards_of).reshape((-1,) + (1,) * (len(extent) - 1 - dim))
    return loudness


def normal_values(key, shape, scale, reach, pieces=(), kind=jnp.bfloat16):
    values = scale * jax.random.normal(key, shape, jnp.float32)
    if pieces:
        values = values * steps_of(key, shape, pieces, -0.22, 0.18)
    return jnp.clip(values, -reach, reach).astype(kind)


def noise_with(rng, extent, deviation, bound, split, heavy, kind=jnp.bfloat16):
    entries = deviation * jax.random.normal(rng, extent, jnp.float32)
    if split:
        entries = entries * steps_of(rng, extent, split, -0.22, 0.18)
    return jnp.clip(strengthened(entries, jax.random.fold_in(rng, 3), *heavy), -bound, bound).astype(kind)


def setup_inputs(seed: int = 0, part: int = 0) -> dict:
    key_of = jax.random.split(jax.random.key(seed), 8)
    part_keys = jax.random.split(jax.random.fold_in(key_of[7], part), 8)
    return {
        "features": noise_with(part_keys[0], (LEN, D), 1.0, 6.0, ((0, 32),), (0, 1, 32, 2.75)),
        "targets": set_ends(jax.random.randint(part_keys[1], (LEN, TRACKS), 0, 4), jax.random.fold_in(part_keys[1], 1), 0, 3).astype(jnp.int32),
        "mappable": set_ends((jax.random.randint(part_keys[2], (LEN,), 0, 8) < 7).astype(jnp.int32), jax.random.fold_in(part_keys[2], 1), 0, 1),
        "w_in": normal_values(key_of[3], (2, D, B), D ** -0.5, 0.21875),
        "w_conv": normal_values(key_of[4], (2, 3, B, B), (3 * B) ** -0.5, 0.1875),
        "w_out": normal_values(key_of[5], (2, B, D), B ** -0.5, 0.3125),
        "w_head": normal_values(key_of[6], (D, TRACKS), (4 * D) ** -0.5, 0.109375),
    }


TANH_COEF = 0.7978845608028654
CUBIC_COEF = 0.044715

def gelu_value(values):
    return jax.nn.gelu(values, approximate=True)

def gelu_slope(values):
    inner = TANH_COEF * (values + CUBIC_COEF * values * values * values)
    tangent = jnp.tanh(inner)
    return 0.5 * (1.0 + tangent) + 0.5 * values * (1.0 - tangent * tangent) * TANH_COEF * (1.0 + 3.0 * CUBIC_COEF * values * values)

def matmul(left, right):
    return jnp.dot(left, right, preferred_element_type=jnp.float32)

def strand_turn(array):
    return jnp.roll(array[::-1], array.shape[1] // 2, axis=1)

def received_earlier(array, shift_amount):
    filler = jnp.zeros((shift_amount, array.shape[1]), array.dtype)
    return jnp.concatenate([filler, array[:-shift_amount]], axis=0)

def from_after(array, shift_amount):
    filler = jnp.zeros((shift_amount, array.shape[1]), array.dtype)
    return jnp.concatenate([array[shift_amount:], filler], axis=0)

def reference(features, targets, mappable, w_in, w_conv, w_out, w_head):
    dilation_list = (FIRST_DILATION, SECOND_DILATION)
    finals = []
    records = []
    for strand in range(2):
        stream = features if strand == 0 else strand_turn(features)
        saved = []
        for layer in range(2):
            shift_amount = dilation_list[layer]
            before_gelu = matmul(stream, w_in[layer])
            hidden = gelu_value(before_gelu).astype(jnp.bfloat16)
            conv_sum = matmul(received_earlier(hidden, shift_amount), w_conv[layer, 0]) + matmul(hidden, w_conv[layer, 1]) + matmul(from_after(hidden, shift_amount), w_conv[layer, 2])
            middle = gelu_value(conv_sum).astype(jnp.bfloat16)
            saved.append((stream, before_gelu, hidden, conv_sum, middle))
            stream = (stream.astype(jnp.float32) + matmul(middle, w_out[layer])).astype(jnp.bfloat16)
        records.append(saved)
        finals.append(stream)
    joined = (0.5 * (finals[0].astype(jnp.float32) + strand_turn(finals[1]).astype(jnp.float32))).astype(jnp.bfloat16)
    logits = matmul(joined, w_head)
    loss_scale = 1.0 / math.sqrt(LEN)
    row_weight = mappable.astype(jnp.float32)[:, None]
    logit_grad = (row_weight * (jnp.exp(logits) - targets.astype(jnp.float32)) * loss_scale).astype(jnp.bfloat16)
    incoming = (0.5 * matmul(logit_grad, w_head.T)).astype(jnp.bfloat16)
    grads_in = [jnp.zeros((D, B), jnp.float32) for layer in range(2)]
    grads_out = [jnp.zeros((B, D), jnp.float32) for layer in range(2)]
    grads_tap = [[jnp.zeros((B, B), jnp.float32) for tap in range(3)] for layer in range(2)]
    for strand in range(2):
        cotangent = incoming if strand == 0 else strand_turn(incoming)
        for layer in (1, 0):
            stream, before_gelu, hidden, conv_sum, middle = records[strand][layer]
            shift_amount = dilation_list[layer]
            grads_out[layer] = grads_out[layer] + matmul(middle.T, cotangent)
            slope_mid = (matmul(cotangent, w_out[layer].T) * gelu_slope(conv_sum)).astype(jnp.bfloat16)
            later = from_after(slope_mid, shift_amount)
            earlier = received_earlier(slope_mid, shift_amount)
            grads_tap[layer][0] = grads_tap[layer][0] + matmul(hidden.T, later)
            grads_tap[layer][1] = grads_tap[layer][1] + matmul(hidden.T, slope_mid)
            grads_tap[layer][2] = grads_tap[layer][2] + matmul(hidden.T, earlier)
            hidden_backward = matmul(later, w_conv[layer, 0].T) + matmul(slope_mid, w_conv[layer, 1].T) + matmul(earlier, w_conv[layer, 2].T)
            slope_in = (hidden_backward * gelu_slope(before_gelu)).astype(jnp.bfloat16)
            grads_in[layer] = grads_in[layer] + matmul(stream.T, slope_in)
            if layer == 1:
                cotangent = (cotangent.astype(jnp.float32) + matmul(slope_in, w_in[layer].T)).astype(jnp.bfloat16)
    grad_in = jnp.stack(grads_in)
    grad_conv = jnp.stack([jnp.stack(grads_tap[layer]) for layer in range(2)])
    grad_out = jnp.stack(grads_out)
    return (grad_in, grad_conv, grad_out)
```

```python
import functools
import math

import jax
import jax.numpy as jnp
from jax import lax
from jax.experimental import pallas as pl
from jax.experimental.pallas import tpu as pltpu
from jax.sharding import PartitionSpec as P

FIRST_DILATION = 2048
SECOND_DILATION = 4096

TANH_COEF = 0.7978845608028654
CUBIC_COEF = 0.044715
LANES = 128
CHUNK = 32
BF16 = jnp.bfloat16
F32 = jnp.float32


def dot(left, right):
    return jnp.dot(left, right, preferred_element_type=F32)


def dot_t(left, right):
    return lax.dot_general(left, right, (((1,), (1,)), ((), ())), preferred_element_type=F32)


def grad_dot(left, right):
    return lax.dot_general(left, right, (((0,), (0,)), ((), ())), preferred_element_type=F32)


def plan(n, hid, channels):
    per_chip = 2 * hid // n
    out = [("out", j, per_chip) for j in range(channels // LANES)]
    conv = [("conv%d" % t, j, per_chip) for t in range(3) for j in range(hid // LANES)]
    inner = [("in", j, 2 * channels // n) for j in range(hid // LANES)]
    segments, start, ends = [], 0, []
    for group in (out, conv, inner):
        for name, column, height in group:
            segments.append((name, column, height, start))
            start += height
        ends.append(start // 32 * 32)
    ends[-1] = -(-start // 32) * 32
    return segments, list(zip([0] + ends[:-1], ends))


def kernel(n, *refs):
    (features, targets, mappable, w_in_hbm, w_conv_hbm, w_out_hbm, w_head_hbm, result) = refs[:8]
    (w_in, w_conv, w_out, w_head, stream, counts_out, counts_in, masks) = refs[8:16]
    (hidden, slope_h, middle, slope_m, cot, grad_v, narrow, wide, joined, logit_grad) = refs[16:26]
    chunk_refs = [refs[26 + 9 * c : 35 + 9 * c] for c in range(3)]
    (weight_sem, a_send, a_recv, g_send, g_recv) = refs[53:]
    rows, channels = features.shape
    hid = w_in.shape[2]
    tracks = w_head.shape[1]
    links = rows * n // FIRST_DILATION
    part = rows // links
    stride = n // links
    me = lax.axis_index("seq")
    high = me // stride
    low = me % stride
    core = low % 2
    bit_x = (low // 2) % 2
    bit_y = low // 4
    first = bit_x * (1 - core) + bit_y * core
    second = bit_y * (1 - core) + bit_x * core
    sibling = me + 1 - 2 * core
    peer_first = me + (1 - 2 * first) * (2 + 2 * core)
    peer_second = me + (1 - 2 * second) * (4 - 2 * core)

    def chain_peer(k):
        return lax.rem(high + k, links) * stride + low

    def remote(src, dst, send, recv, peer):
        return pltpu.make_async_remote_copy(
            src_ref=src,
            dst_ref=dst,
            send_sem=send,
            recv_sem=recv,
            device_id={"seq": peer},
            device_id_type=pl.DeviceIdType.MESH,
        )

    weight_copies = [
        pltpu.make_async_copy(src, dst, weight_sem.at[i])
        for i, (src, dst) in enumerate(
            ((w_head_hbm, w_head), (w_in_hbm, w_in), (w_conv_hbm, w_conv), (w_out_hbm, w_out))
        )
    ]
    for copy in weight_copies:
        copy.start()

    barrier = pltpu.get_barrier_semaphore()
    partners = [sibling, peer_first, peer_second] + [chain_peer(k) for k in range(1, links)]
    for peer in partners:
        pl.semaphore_signal(
            barrier, inc=1, device_id={"seq": peer}, device_id_type=pl.DeviceIdType.MESH
        )

    def chunks(count, body):
        def step(i, carry):
            body(pl.ds(pl.multiple_of(i * CHUNK, CHUNK), CHUNK))
            return carry

        lax.fori_loop(0, count // CHUNK, step, 0)

    loss_scale = 1.0 / math.sqrt(rows * n)
    mask_row = mappable[...].astype(F32)
    masks[high] = jnp.broadcast_to(mask_row, masks.shape[1:])

    def mask_of(p, first_row, count):
        lane = lax.broadcasted_iota(jnp.int32, (count, rows), 1)
        row = lax.broadcasted_iota(jnp.int32, (count, rows), 0)
        values = jnp.broadcast_to(masks[p, :1, :], (count, rows))
        return jnp.sum(jnp.where(lane == row + first_row, values, 0.0), axis=1, keepdims=True)

    pl.semaphore_wait(barrier, len(partners))

    own = pl.ds(pl.multiple_of(high * part, part), part)
    regroup = [[], [], []]

    def send_parts(which, src, dst):
        for k in range(1, links):
            there = pl.ds(pl.multiple_of(lax.rem(high + k, links) * part, part), part)
            copy = remote(
                src.at[there], dst.at[own], a_send.at[which, k], a_recv.at[which, k], chain_peer(k)
            )
            copy.start()
            regroup[which].append(copy)
        dst[own, :] = src[own, :]

    send_parts(0, features, stream.at[0])
    for k in range(1, links):
        copy = remote(masks.at[high], masks.at[high], a_send.at[2, k], a_recv.at[2, k], chain_peer(k))
        copy.start()
        regroup[2].append(copy)
    weight_copies[0].wait()
    logit_grad[...] = (targets[...].astype(F32) * mask_of(high, 0, rows)).astype(BF16)
    counts_out[...] = (dot_t(logit_grad[...], w_head[...]) * (0.5 * loss_scale)).astype(BF16)
    send_parts(1, counts_out, counts_in)

    def swap(value):
        half = value.shape[1] // 2
        return jnp.concatenate([value[:, half:], value[:, :half]], axis=1)

    def mirror(p):
        return rows + (links - 1 - p) * part

    def chain_chunks(body):
        for p in range(links):

            def step(i, carry, p=p):
                offset = pl.multiple_of(i * CHUNK, CHUNK)
                body(pl.ds(p * part + offset, CHUNK), pl.ds(mirror(p) + offset, CHUNK))
                return carry

            lax.fori_loop(0, part // CHUNK, step, 0)

    def activate(value_ref, slope_ref, layer):
        def body(at):
            v = narrow[at, :]
            square = v * v
            tangent = jnp.tanh(TANH_COEF * (v + CUBIC_COEF * square * v))
            value_ref[layer, at, :] = (0.5 * v * (1.0 + tangent)).astype(BF16)
            slope_ref[layer, at, :] = 0.5 * (1.0 + tangent) + 0.5 * v * (
                1.0 - tangent * tangent
            ) * TANH_COEF * (1.0 + 3.0 * CUBIC_COEF * square)

        chunks(2 * rows, body)

    def strand(s):
        return slice(s * rows, (s + 1) * rows)

    def ends(s, skip):
        return slice(s * rows + skip, (s + 1) * rows), slice(s * rows, (s + 1) * rows - skip)

    steps_of = (1, SECOND_DILATION // FIRST_DILATION)

    for copy in regroup[0]:
        copy.wait()

    def spread(at, across):
        stream[0, across, :] = swap(stream[0, at, :])

    chain_chunks(spread)
    for copy in weight_copies[1:]:
        copy.wait()

    for layer in range(2):
        skip = steps_of[layer] * part
        for s in range(2):
            narrow[strand(s), :] = dot(stream[layer, strand(s), :], w_in[layer])
        activate(hidden, slope_h, layer)
        for s in range(2):
            narrow[strand(s), :] = dot(hidden[layer, strand(s), :], w_conv[layer, 1])
            after, before = ends(s, skip)
            narrow[after, :] += dot(hidden[layer, before, :], w_conv[layer, 0])
            narrow[before, :] += dot(hidden[layer, after, :], w_conv[layer, 2])
        activate(middle, slope_m, layer)
        for s in range(2):
            wide[strand(s), :] = dot(middle[layer, strand(s), :], w_out[layer])

        def add(at, layer=layer):
            stream[layer + 1, at, :] = (stream[layer, at, :].astype(F32) + wide[at, :]).astype(BF16)

        chunks(2 * rows, add)

    def join(at, across):
        joined[at, :] = (
            0.5 * (stream[2, at, :].astype(F32) + swap(stream[2, across, :]).astype(F32))
        ).astype(BF16)

    chain_chunks(join)
    for copy in regroup[2]:
        copy.wait()
    mask = jnp.concatenate([mask_of(p, high * part, part) for p in range(links)], axis=0) * loss_scale
    for panel in range(tracks // LANES):
        at_panel = slice(panel * LANES, (panel + 1) * LANES)
        logits = dot(joined[...], w_head[:, at_panel])
        logit_grad[:, at_panel] = (mask * jnp.exp(logits)).astype(BF16)
    wide[:rows, :] = dot_t(logit_grad[...], w_head[...])
    for copy in regroup[1]:
        copy.wait()

    def divide(at, across):
        incoming = (0.5 * wide[at, :] - counts_in[at, :].astype(F32)).astype(BF16)
        cot[at, :] = incoming
        cot[across, :] = swap(incoming)

    chain_chunks(divide)

    quads = [(h, y, x) for h in range(links) for y in range(2) for x in range(2)]
    segments, chunk_ends = plan(n, hid, channels)
    values = [{}, {}]

    def place(layer, chunk):
        begin, end = chunk_ends[chunk]
        half_rows = (end - begin) // 2
        for half in range(2):
            low_row, high_row = begin + half * half_rows, begin + (half + 1) * half_rows
            for j, (h, y, x) in enumerate(quads):
                b, a = (y, x) if half == 0 else (x, y)
                pieces, filled = [], 0
                for name, column, height, start in segments:
                    first_row, last_row = max(start, low_row), min(start + height, high_row)
                    if first_row >= last_row:
                        continue
                    base = j * height - start
                    at_column = slice(column * LANES, (column + 1) * LANES)
                    pieces.append(
                        values[layer][name][base + first_row : base + last_row, at_column]
                    )
                    filled += last_row - first_row
                if filled < half_rows:
                    pieces.append(jnp.zeros((half_rows - filled, LANES), F32))
                block = pieces[0] if len(pieces) == 1 else jnp.concatenate(pieces, axis=0)
                chunk_refs[chunk][0][layer, half, h, b, a] = block.astype(BF16)

    class Scatter:
        def __init__(self, layer, chunk):
            (self.sums, self.recv0, *pairs, self.final) = chunk_refs[chunk]
            self.send, self.recv = [None] + pairs[0::2], [self.recv0] + pairs[1::2]
            self.layer, self.index = layer, 3 * layer + chunk
            self.stage, self.copies = 0, []

        def start(self, src, dst, sem, peer):
            copy = remote(src, dst, g_send.at[self.index, sem], g_recv.at[self.index, sem], peer)
            copy.start()
            self.copies.append(copy)

        def finish(self):
            for copy in self.copies:
                copy.wait()
            self.copies = []

        def advance(self):
            self.finish()
            getattr(self, "stage%d" % self.stage)()
            self.stage += 1

        def stage0(self):
            self.start(
                self.sums.at[self.layer, 1 - core], self.recv[0].at[self.layer], 0, sibling
            )

        def partial0(self, h, b, a):
            return self.sums[self.layer, core, h, b, a].astype(F32) + self.recv[0][
                self.layer, h, b, a
            ].astype(F32)

        def partial1(self, h, b):
            return self.partial0(h, b, first) + self.recv[1][self.layer, h, b].astype(F32)

        def partial2(self, h):
            return self.partial1(h, second) + self.recv[2][self.layer, h].astype(F32)

        def stage1(self):
            def step(h, carry):
                for b in range(2):
                    self.send[1][self.layer, h, b] = self.partial0(h, b, 1 - first).astype(BF16)
                return carry

            lax.fori_loop(0, links, step, 0)
            self.start(self.send[1].at[self.layer], self.recv[1].at[self.layer], 1, peer_first)

        def stage2(self):
            def step(h, carry):
                self.send[2][self.layer, h] = self.partial1(h, 1 - second).astype(BF16)
                return carry

            lax.fori_loop(0, links, step, 0)
            self.start(self.send[2].at[self.layer], self.recv[2].at[self.layer], 2, peer_second)

        def stage3(self):
            for k in range(1, links):
                self.send[3][self.layer, k] = self.partial2(lax.rem(high + k, links)).astype(BF16)
                self.start(
                    self.send[3].at[self.layer, k],
                    self.recv[3].at[self.layer, k],
                    3 + k,
                    chain_peer(k),
                )

        def stage4(self):
            total = self.partial2(high)
            for k in range(1, links):
                total = total + self.recv[3][self.layer, k].astype(F32)
            self.final[self.layer, core] = total
            here = self.final.at[self.layer, core]
            self.start(here, here, 3, sibling)

    scatters = [[Scatter(layer, chunk) for chunk in range(3)] for layer in range(2)]

    def advance(*which):
        for layer, chunk in which:
            scatters[layer][chunk].advance()

    for layer in (1, 0):
        skip = steps_of[layer] * part
        values[layer]["out"] = grad_dot(middle[layer], cot[...])
        place(layer, 0)
        advance((layer, 0))
        for s in range(2):
            narrow[strand(s), :] = dot_t(cot[strand(s), :], w_out[layer])

        def slope(at, layer=layer):
            grad_v[at, :] = (narrow[at, :] * slope_m[layer, at, :]).astype(BF16)

        chunks(2 * rows, slope)
        advance((layer, 0))
        if layer == 0:
            advance((1, 1))
        spans = [ends(s, skip) for s in range(2)]

        def joined_rows(read, side):
            return jnp.concatenate([read(spans[s][side]) for s in range(2)], axis=0)

        def read_hidden(at, layer=layer):
            return hidden[layer, at, :]

        def read_grad(at):
            return grad_v[at, :]

        values[layer]["conv0"] = grad_dot(joined_rows(read_hidden, 1), joined_rows(read_grad, 0))
        values[layer]["conv1"] = grad_dot(hidden[layer], grad_v[...])
        values[layer]["conv2"] = grad_dot(joined_rows(read_hidden, 0), joined_rows(read_grad, 1))
        place(layer, 1)
        advance((layer, 1))
        for s in range(2):
            narrow[strand(s), :] = dot_t(grad_v[strand(s), :], w_conv[layer, 1])
            after, before = ends(s, skip)
            narrow[before, :] += dot_t(grad_v[after, :], w_conv[layer, 0])
            narrow[after, :] += dot_t(grad_v[before, :], w_conv[layer, 2])

        def slope_back(at, layer=layer):
            grad_v[at, :] = (narrow[at, :] * slope_h[layer, at, :]).astype(BF16)

        chunks(2 * rows, slope_back)
        advance((layer, 1))
        if layer == 0:
            advance((1, 0))
        values[layer]["in"] = grad_dot(stream[layer], grad_v[...])
        place(layer, 2)
        advance((layer, 2))
        if layer == 1:
            for s in range(2):
                wide[strand(s), :] = dot_t(grad_v[strand(s), :], w_in[layer])

            def renew(at):
                cot[at, :] = (cot[at, :].astype(F32) + wide[at, :]).astype(BF16)

            chunks(2 * rows, renew)
            advance((1, 2), (1, 0))
    advance((1, 2), (0, 2))
    advance((1, 1), (0, 0), (1, 0), (1, 2), (1, 1), (0, 1), (0, 0), (1, 2), (0, 2))
    advance((0, 1), (0, 0), (0, 2), (0, 1), (0, 2))
    for layer in (1, 0):
        for chunk, (begin, end) in enumerate(chunk_ends):
            scatter = scatters[layer][chunk]
            assert scatter.stage == 5
            scatter.finish()
            middle_row = (begin + end) // 2
            result[layer, begin:middle_row, :] = scatter.final[layer, 0]
            result[layer, middle_row:end, :] = scatter.final[layer, 1]


def deliver(n, result, out_in, out_conv, out_out):
    core = lax.axis_index("seq") % 2
    segments, _ = plan(n, out_conv.shape[3], out_out.shape[2])
    for c in range(2):

        @pl.when(core == c)
        def _(c=c):
            for layer in range(2):
                for name, column, height, start in segments:
                    own = height // 2
                    value = result[layer, start + c * own : start + (c + 1) * own, :]
                    lanes = slice(column * LANES, (column + 1) * LANES)
                    if name == "in":
                        out_in[layer, :, lanes] = value
                    elif name == "out":
                        out_out[:, layer, lanes] = value
                    else:
                        out_conv[int(name[-1]), :, layer, lanes] = value


def local(features, targets, mappable, w_in, w_conv, w_out, w_head):
    rows, channels = features.shape
    n = lax.axis_size("seq")
    links = rows * n // FIRST_DILATION
    hid = w_in.shape[2]
    tracks = targets.shape[1]
    both = 2 * rows
    vmem = pl.BlockSpec(memory_space=pltpu.VMEM)
    hbm = pl.BlockSpec(memory_space=pl.ANY)
    chunk_shapes = []
    _, chunk_ends = plan(n, hid, channels)
    for begin, end in chunk_ends:
        block = ((end - begin) // 2, LANES)
        chunk_shapes += [
            pltpu.VMEM((2, 2, links, 2, 2) + block, BF16),
            pltpu.VMEM((2, links, 2, 2) + block, BF16),
            pltpu.VMEM((2, links, 2) + block, BF16),
            pltpu.VMEM((2, links, 2) + block, BF16),
            pltpu.VMEM((2, links) + block, BF16),
            pltpu.VMEM((2, links) + block, BF16),
            pltpu.VMEM((2, links) + block, BF16),
            pltpu.VMEM((2, links) + block, BF16),
            pltpu.VMEM((2, 2) + block, F32),
        ]
    result = pl.pallas_call(
        functools.partial(kernel, n),
        out_shape=jax.ShapeDtypeStruct((2, chunk_ends[-1][1], LANES), F32),
        in_specs=[vmem, vmem, vmem, hbm, hbm, hbm, hbm],
        out_specs=vmem,
        scratch_shapes=[
            pltpu.VMEM(w_in.shape, BF16),
            pltpu.VMEM(w_conv.shape, BF16),
            pltpu.VMEM(w_out.shape, BF16),
            pltpu.VMEM(w_head.shape, BF16),
            pltpu.VMEM((3, both, channels), BF16),
            pltpu.VMEM((rows, channels), BF16),
            pltpu.VMEM((rows, channels), BF16),
            pltpu.VMEM((links, 8, rows), F32),
            pltpu.VMEM((2, both, hid), BF16),
            pltpu.VMEM((2, both, hid), F32),
            pltpu.VMEM((2, both, hid), BF16),
            pltpu.VMEM((2, both, hid), F32),
            pltpu.VMEM((both, channels), BF16),
            pltpu.VMEM((both, hid), BF16),
            pltpu.VMEM((both, hid), F32),
            pltpu.VMEM((both, channels), F32),
            pltpu.VMEM((rows, channels), BF16),
            pltpu.VMEM((rows, tracks), BF16),
            *chunk_shapes,
            pltpu.SemaphoreType.DMA((4,)),
            pltpu.SemaphoreType.DMA((3, links)),
            pltpu.SemaphoreType.DMA((3, links)),
            pltpu.SemaphoreType.DMA((6, 3 + links)),
            pltpu.SemaphoreType.DMA((6, 3 + links)),
        ],
        compiler_params=pltpu.CompilerParams(
            collective_id=0, has_side_effects=True, vmem_limit_bytes=60 * 1024 * 1024
        ),
    )(features, targets, mappable[None, :], w_in, w_conv, w_out, w_head)
    grad_in, grad_conv, grad_out = pl.pallas_call(
        functools.partial(deliver, n),
        out_shape=(
            jax.ShapeDtypeStruct((2, channels // n, hid), F32),
            jax.ShapeDtypeStruct((3, hid // n, 2, hid), F32),
            jax.ShapeDtypeStruct((hid // n, 2, channels), F32),
        ),
        in_specs=[vmem],
        out_specs=(vmem, vmem, vmem),
    )(result)
    return (grad_in, jnp.transpose(grad_conv, (2, 0, 1, 3)), jnp.transpose(grad_out, (1, 0, 2)))


def solution(mesh):
    in_specs = (
        P(("grp", "seq"), None),
        P(("grp", "seq"), None),
        P(("grp", "seq")),
        P(),
        P(),
        P(),
        P(),
    )
    out_specs = (P("grp", "seq", None), P("grp", None, "seq", None), P("grp", "seq", None))
    return jax.shard_map(local, mesh=mesh, in_specs=in_specs, out_specs=out_specs, check_vma=False)
```

```python
import functools
import math

import jax
import jax.numpy as jnp
from jax import lax
from jax.experimental import pallas as pl
from jax.experimental.pallas import tpu as pltpu
from jax.sharding import PartitionSpec as P

FIRST_DILATION = 2048
SECOND_DILATION = 4096

TANH_COEF = 0.7978845608028654
CUBIC_COEF = 0.044715
LANES = 128
CHUNK = 32
BF16 = jnp.bfloat16
F32 = jnp.float32


def dot(left, right):
    return jnp.dot(left, right, preferred_element_type=F32)


def dot_t(left, right):
    return lax.dot_general(left, right, (((1,), (1,)), ((), ())), preferred_element_type=F32)


def grad_dot(left, right):
    return lax.dot_general(left, right, (((0,), (0,)), ((), ())), preferred_element_type=F32)


def plan(n, hid, channels):
    per_chip = 2 * hid // n
    out = [("out", j, per_chip) for j in range(channels // LANES)]
    conv = [("conv%d" % t, j, per_chip) for t in range(3) for j in range(hid // LANES)]
    inner = [("in", j, 2 * channels // n) for j in range(hid // LANES)]
    segments, start, ends = [], 0, []
    for group in (out, conv, inner):
        for name, column, height in group:
            segments.append((name, column, height, start))
            start += height
        ends.append(start // 32 * 32)
    ends[-1] = -(-start // 32) * 32
    return segments, list(zip([0] + ends[:-1], ends))


def kernel(n, *refs):
    (features, targets_hbm, mappable_hbm, w_in_hbm, w_conv_hbm, w_out_hbm, w_head_hbm, result) = refs[:8]
    (w_in, w_conv, w_out, w_head, stream, counts_out, counts_in, masks) = refs[8:16]
    (hidden, slope_h, middle, slope_m, cot, grad_v, narrow, wide, joined, logit_grad) = refs[16:26]
    chunk_refs = [refs[26 + 8 * c : 34 + 8 * c] for c in range(3)]
    (quad_send, quad_recv, targets, mappable) = refs[50:54]
    (weight_sem, a_send, a_recv, g_send, g_recv) = refs[54:]
    rows, channels = features.shape
    hid = w_in.shape[2]
    tracks = w_head.shape[1]
    links = rows * n // FIRST_DILATION
    part = rows // links
    stride = n // links
    me = lax.axis_index("seq")
    high = me // stride
    low = me % stride
    core = low % 2
    bit_x = (low // 2) % 2
    bit_y = low // 4
    first = bit_x * (1 - core) + bit_y * core
    second = bit_y * (1 - core) + bit_x * core
    sibling = me + 1 - 2 * core
    peer_first = me + (1 - 2 * first) * (2 + 2 * core)
    peer_second = me + (1 - 2 * second) * (4 - 2 * core)

    def chain_peer(k):
        return lax.rem(high + k, links) * stride + low

    def remote(src, dst, send, recv, peer):
        return pltpu.make_async_remote_copy(
            src_ref=src,
            dst_ref=dst,
            send_sem=send,
            recv_sem=recv,
            device_id={"seq": peer},
            device_id_type=pl.DeviceIdType.MESH,
        )

    peer_across = peer_first + peer_second - me
    weight_copies = [
        pltpu.make_async_copy(src, dst, weight_sem.at[i])
        for i, (src, dst) in enumerate(
            ((mappable_hbm, mappable), (targets_hbm, targets), (w_head_hbm, w_head), (w_in_hbm, w_in), (w_conv_hbm, w_conv), (w_out_hbm, w_out))
        )
    ]
    for copy in weight_copies:
        copy.start()

    barrier = pltpu.get_barrier_semaphore()
    partners = [sibling, peer_first, peer_second, peer_across] + [chain_peer(k) for k in range(1, links)]
    for peer in partners:
        pl.semaphore_signal(
            barrier, inc=1, device_id={"seq": peer}, device_id_type=pl.DeviceIdType.MESH
        )

    def chunks(count, body):
        def step(i, carry):
            body(pl.ds(pl.multiple_of(i * CHUNK, CHUNK), CHUNK))
            return carry

        lax.fori_loop(0, count // CHUNK, step, 0, unroll=True)

    loss_scale = 1.0 / math.sqrt(rows * n)
    def mask_of(p, first_row, count):
        lane = lax.broadcasted_iota(jnp.int32, (count, rows), 1)
        row = lax.broadcasted_iota(jnp.int32, (count, rows), 0)
        values = jnp.broadcast_to(masks[p, :1, :], (count, rows))
        return jnp.sum(jnp.where(lane == row + first_row, values, 0.0), axis=1, keepdims=True)

    pl.semaphore_wait(barrier, len(partners))

    own = pl.ds(pl.multiple_of(high * part, part), part)
    regroup = [[], [], []]

    def send_parts(which, src, dst):
        for k in range(1, links):
            there = pl.ds(pl.multiple_of(lax.rem(high + k, links) * part, part), part)
            copy = remote(
                src.at[there], dst.at[own], a_send.at[which, k], a_recv.at[which, k], chain_peer(k)
            )
            copy.start()
            regroup[which].append(copy)

    send_parts(0, features, stream.at[0])
    own_copy = pltpu.make_async_copy(features.at[own], stream.at[0, own], weight_sem.at[6])
    own_copy.start()
    weight_copies[0].wait()
    masks[high] = jnp.broadcast_to(mappable[...].astype(F32), masks.shape[1:])
    for k in range(1, links):
        copy = remote(masks.at[high], masks.at[high], a_send.at[2, k], a_recv.at[2, k], chain_peer(k))
        copy.start()
        regroup[2].append(copy)
    weight_copies[1].wait()
    logit_grad[...] = (targets[...].astype(F32) * mask_of(high, 0, rows)).astype(BF16)
    weight_copies[2].wait()
    counts_out[...] = (dot_t(logit_grad[...], w_head[...]) * (0.5 * loss_scale)).astype(BF16)
    counts_in[own, :] = counts_out[own, :]
    for copy in regroup[0]:
        copy.wait_send()
    send_parts(1, counts_out, counts_in)

    def swap(value):
        half = value.shape[1] // 2
        return jnp.concatenate([value[:, half:], value[:, :half]], axis=1)

    def mirror(p):
        return rows + (links - 1 - p) * part

    def chain_chunks(body):
        for p in range(links):

            def step(i, carry, p=p):
                offset = pl.multiple_of(i * CHUNK, CHUNK)
                body(pl.ds(p * part + offset, CHUNK), pl.ds(mirror(p) + offset, CHUNK))
                return carry

            lax.fori_loop(0, part // CHUNK, step, 0, unroll=True)

    def activate(value_ref, slope_ref, layer):
        def body(at):
            v = narrow[at, :]
            square = v * v
            tangent = jnp.tanh(TANH_COEF * (v + CUBIC_COEF * square * v))
            value_ref[layer, at, :] = (0.5 * v * (1.0 + tangent)).astype(BF16)
            slope_ref[layer, at, :] = 0.5 * (1.0 + tangent) + 0.5 * v * (
                1.0 - tangent * tangent
            ) * TANH_COEF * (1.0 + 3.0 * CUBIC_COEF * square)

        chunks(2 * rows, body)

    def strand(s):
        return slice(s * rows, (s + 1) * rows)

    def ends(s, skip):
        return slice(s * rows + skip, (s + 1) * rows), slice(s * rows, (s + 1) * rows - skip)

    steps_of = (1, SECOND_DILATION // FIRST_DILATION)

    own_copy.wait()
    for copy in regroup[0]:
        copy.wait_recv()

    def spread(at, across):
        stream[0, across, :] = swap(stream[0, at, :])

    chain_chunks(spread)
    for copy in weight_copies[3:]:
        copy.wait()

    for layer in range(2):
        skip = steps_of[layer] * part
        for s in range(2):
            narrow[strand(s), :] = dot(stream[layer, strand(s), :], w_in[layer])
        activate(hidden, slope_h, layer)
        for s in range(2):
            narrow[strand(s), :] = dot(hidden[layer, strand(s), :], w_conv[layer, 1])
            after, before = ends(s, skip)
            narrow[after, :] += dot(hidden[layer, before, :], w_conv[layer, 0])
            narrow[before, :] += dot(hidden[layer, after, :], w_conv[layer, 2])
        activate(middle, slope_m, layer)
        for s in range(2):
            wide[strand(s), :] = dot(middle[layer, strand(s), :], w_out[layer])

        def add(at, layer=layer):
            stream[layer + 1, at, :] = (stream[layer, at, :].astype(F32) + wide[at, :]).astype(BF16)

        chunks(2 * rows, add)

    def join(at, across):
        joined[at, :] = (
            0.5 * (stream[2, at, :].astype(F32) + swap(stream[2, across, :]).astype(F32))
        ).astype(BF16)

    chain_chunks(join)
    for copy in regroup[2]:
        copy.wait()
    mask = jnp.concatenate([mask_of(p, high * part, part) for p in range(links)], axis=0) * loss_scale
    for panel in range(tracks // LANES):
        at_panel = slice(panel * LANES, (panel + 1) * LANES)
        logits = dot(joined[...], w_head[:, at_panel])
        logit_grad[:, at_panel] = (mask * jnp.exp(logits)).astype(BF16)
    wide[:rows, :] = dot_t(logit_grad[...], w_head[...])
    for copy in regroup[1]:
        copy.wait()

    def divide(at, across):
        incoming = (0.5 * wide[at, :] - counts_in[at, :].astype(F32)).astype(BF16)
        cot[at, :] = incoming
        cot[across, :] = swap(incoming)

    chain_chunks(divide)

    quads = [(h, y, x) for h in range(links) for y in range(2) for x in range(2)]
    segments, chunk_ends = plan(n, hid, channels)
    values = [{}, {}]

    def place(layer, chunk):
        begin, end = chunk_ends[chunk]
        half_rows = (end - begin) // 2
        for half in range(2):
            low_row, high_row = begin + half * half_rows, begin + (half + 1) * half_rows
            for j, (h, y, x) in enumerate(quads):
                b, a = (y, x) if half == 0 else (x, y)
                pieces, filled = [], 0
                for name, column, height, start in segments:
                    first_row, last_row = max(start, low_row), min(start + height, high_row)
                    if first_row >= last_row:
                        continue
                    base = j * height - start
                    at_column = slice(column * LANES, (column + 1) * LANES)
                    pieces.append(
                        values[layer][name][base + first_row : base + last_row, at_column]
                    )
                    filled += last_row - first_row
                if filled < half_rows:
                    pieces.append(jnp.zeros((half_rows - filled, LANES), F32))
                block = pieces[0] if len(pieces) == 1 else jnp.concatenate(pieces, axis=0)
                chunk_refs[chunk][0][layer, half, h, b, a] = block.astype(BF16)

    class Scatter:
        def __init__(self, layer, chunk):
            (self.sums, self.recv0, *pairs) = chunk_refs[chunk]
            begin, end = chunk_ends[chunk]
            self.half = (end - begin) // 2
            self.own = pl.ds(pl.multiple_of(begin + core * self.half, 16), self.half)
            self.send, self.recv = [None] + pairs[0::2], [self.recv0] + pairs[1::2]
            self.layer, self.index = layer, 3 * layer + chunk
            self.stage, self.copies = 0, []

        def start(self, src, dst, sem, peer):
            copy = remote(src, dst, g_send.at[self.index, sem], g_recv.at[self.index, sem], peer)
            copy.start()
            self.copies.append(copy)

        def finish(self):
            for copy in self.copies:
                copy.wait()
            self.copies = []

        def advance(self):
            self.finish()
            getattr(self, "stage%d" % self.stage)()
            self.stage += 1

        def stage0(self):
            self.start(
                self.sums.at[self.layer, 1 - core], self.recv[0].at[self.layer], 0, sibling
            )

        def partial0(self, h, b, a):
            return self.sums[self.layer, core, h, b, a].astype(F32) + self.recv[0][
                self.layer, h, b, a
            ].astype(F32)

        def partial1(self, h, b):
            return self.partial0(h, b, first) + self.recv[1][self.layer, h, b].astype(F32)

        def partial2(self, h):
            return self.partial1(h, second) + self.recv[2][self.layer, h].astype(F32)

        def stage1(self):
            def step(h, carry):
                for b in range(2):
                    self.send[1][self.layer, h, b] = self.partial0(h, b, 1 - first).astype(BF16)
                return carry

            lax.fori_loop(0, links, step, 0, unroll=True)
            self.start(self.send[1].at[self.layer], self.recv[1].at[self.layer], 1, peer_first)

        def stage2(self):
            def step(h, carry):
                self.send[2][self.layer, h] = self.partial1(h, 1 - second).astype(BF16)
                return carry

            lax.fori_loop(0, links, step, 0, unroll=True)
            self.start(self.send[2].at[self.layer], self.recv[2].at[self.layer], 2, peer_second)

        def stage3(self):
            for k in range(1, links):
                self.send[3][self.layer, k] = self.partial2(lax.rem(high + k, links)).astype(BF16)
                self.start(
                    self.send[3].at[self.layer, k],
                    self.recv[3].at[self.layer, k],
                    3 + k,
                    chain_peer(k),
                )

        def stage4(self):
            total = self.partial2(high)
            for k in range(1, links):
                total = total + self.recv[3][self.layer, k].astype(F32)
            result[self.layer, self.own, :] = total
            here = result.at[self.layer, self.own]
            self.start(here, here, 3, sibling)

    class QuadScatter(Scatter):
        def stage1(self):
            places = ((second, 1 - first), (1 - second, first), (1 - second, 1 - first))
            peers = (peer_first, peer_second, peer_across)
            for m, ((b, a), peer) in enumerate(zip(places, peers)):
                for h in range(links):
                    quad_send[m, h] = self.partial0(h, b, a).astype(BF16)
                self.start(quad_send.at[m], quad_recv.at[m], (1, 2, 3 + links)[m], peer)
            self.stage += 1

        def partial2(self, h):
            total = self.partial0(h, second, first)
            for m in range(3):
                total = total + quad_recv[m, h].astype(F32)
            return total

    scatters = [[Scatter(layer, chunk) for chunk in range(3)] for layer in range(2)]
    scatters[0][2] = QuadScatter(0, 2)

    def advance(*which):
        for layer, chunk in which:
            scatters[layer][chunk].advance()

    def grads_out(layer):
        values[layer]["out"] = grad_dot(middle[layer], cot[...])
        place(layer, 0)

    def slopes_mid(layer):
        for s in range(2):
            narrow[strand(s), :] = dot_t(cot[strand(s), :], w_out[layer])

        def slope(at):
            grad_v[at, :] = (narrow[at, :] * slope_m[layer, at, :]).astype(BF16)

        chunks(2 * rows, slope)

    def grads_conv(layer):
        spans = [ends(s, steps_of[layer] * part) for s in range(2)]

        def joined_rows(read, side):
            return jnp.concatenate([read(spans[s][side]) for s in range(2)], axis=0)

        def read_hidden(at):
            return hidden[layer, at, :]

        def read_grad(at):
            return grad_v[at, :]

        values[layer]["conv0"] = grad_dot(joined_rows(read_hidden, 1), joined_rows(read_grad, 0))
        values[layer]["conv1"] = grad_dot(hidden[layer], grad_v[...])
        values[layer]["conv2"] = grad_dot(joined_rows(read_hidden, 0), joined_rows(read_grad, 1))
        place(layer, 1)

    def slopes_in(layer):
        for s in range(2):
            narrow[strand(s), :] = dot_t(grad_v[strand(s), :], w_conv[layer, 1])
            after, before = ends(s, steps_of[layer] * part)
            narrow[before, :] += dot_t(grad_v[after, :], w_conv[layer, 0])
            narrow[after, :] += dot_t(grad_v[before, :], w_conv[layer, 2])

        def slope_back(at):
            grad_v[at, :] = (narrow[at, :] * slope_h[layer, at, :]).astype(BF16)

        chunks(2 * rows, slope_back)

    def grads_in(layer):
        values[layer]["in"] = grad_dot(stream[layer], grad_v[...])
        place(layer, 2)

    def renew_cot():
        for s in range(2):
            wide[strand(s), :] = dot_t(grad_v[strand(s), :], w_in[1])

        def renew(at):
            cot[at, :] = (cot[at, :].astype(F32) + wide[at, :]).astype(BF16)

        chunks(2 * rows, renew)

    grads_out(1)
    advance((1, 0))
    slopes_mid(1)
    grads_conv(1)
    advance((1, 1), (1, 0))
    slopes_in(1)
    grads_in(1)
    advance((1, 2), (1, 1))
    renew_cot()
    grads_out(0)
    advance((0, 0), (1, 2))
    slopes_mid(0)
    grads_conv(0)
    advance((0, 1), (0, 0), (1, 0))
    slopes_in(0)
    grads_in(0)
    advance((0, 2), (0, 1))
    advance((1, 1), (0, 2), (1, 0), (1, 2), (0, 0), (1, 1), (1, 0), (0, 1), (1, 2), (0, 0), (1, 1), (0, 2))
    advance((1, 2), (0, 1), (0, 0), (0, 2), (0, 1))
    for layer in (1, 0):
        for scatter in scatters[layer]:
            assert scatter.stage == 5
            scatter.finish()


def deliver(n, result, out_in, out_conv, out_out):
    core = lax.axis_index("seq") % 2
    segments, _ = plan(n, out_conv.shape[3], out_out.shape[2])
    for c in range(2):

        @pl.when(core == c)
        def _(c=c):
            for layer in range(2):
                for name, column, height, start in segments:
                    own = height // 2
                    value = result[layer, start + c * own : start + (c + 1) * own, :]
                    lanes = slice(column * LANES, (column + 1) * LANES)
                    if name == "in":
                        out_in[layer, :, lanes] = value
                    elif name == "out":
                        out_out[:, layer, lanes] = value
                    else:
                        out_conv[int(name[-1]), :, layer, lanes] = value


def local(features, targets, mappable, w_in, w_conv, w_out, w_head):
    rows, channels = features.shape
    n = lax.axis_size("seq")
    links = rows * n // FIRST_DILATION
    hid = w_in.shape[2]
    tracks = targets.shape[1]
    both = 2 * rows
    vmem = pl.BlockSpec(memory_space=pltpu.VMEM)
    hbm = pl.BlockSpec(memory_space=pl.ANY)
    chunk_shapes = []
    _, chunk_ends = plan(n, hid, channels)
    for begin, end in chunk_ends:
        block = ((end - begin) // 2, LANES)
        chunk_shapes += [
            pltpu.VMEM((2, 2, links, 2, 2) + block, BF16),
            pltpu.VMEM((2, links, 2, 2) + block, BF16),
            pltpu.VMEM((2, links, 2) + block, BF16),
            pltpu.VMEM((2, links, 2) + block, BF16),
            pltpu.VMEM((2, links) + block, BF16),
            pltpu.VMEM((2, links) + block, BF16),
            pltpu.VMEM((2, links) + block, BF16),
            pltpu.VMEM((2, links) + block, BF16),
        ]
    result = pl.pallas_call(
        functools.partial(kernel, n),
        out_shape=jax.ShapeDtypeStruct((2, chunk_ends[-1][1], LANES), F32),
        in_specs=[hbm] * 7,
        out_specs=vmem,
        scratch_shapes=[
            pltpu.VMEM(w_in.shape, BF16),
            pltpu.VMEM(w_conv.shape, BF16),
            pltpu.VMEM(w_out.shape, BF16),
            pltpu.VMEM(w_head.shape, BF16),
            pltpu.VMEM((3, both, channels), BF16),
            pltpu.VMEM((rows, channels), BF16),
            pltpu.VMEM((rows, channels), BF16),
            pltpu.VMEM((links, 8, rows), F32),
            pltpu.VMEM((2, both, hid), BF16),
            pltpu.VMEM((2, both, hid), F32),
            pltpu.VMEM((2, both, hid), BF16),
            pltpu.VMEM((2, both, hid), F32),
            pltpu.VMEM((both, channels), BF16),
            pltpu.VMEM((both, hid), BF16),
            pltpu.VMEM((both, hid), F32),
            pltpu.VMEM((both, channels), F32),
            pltpu.VMEM((rows, channels), BF16),
            pltpu.VMEM((rows, tracks), BF16),
            *chunk_shapes,
            pltpu.VMEM((3, links) + block, BF16),
            pltpu.VMEM((3, links) + block, BF16),
            pltpu.VMEM((rows, tracks), jnp.int32),
            pltpu.VMEM((1, rows), jnp.int32),
            pltpu.SemaphoreType.DMA((7,)),
            pltpu.SemaphoreType.DMA((3, links)),
            pltpu.SemaphoreType.DMA((3, links)),
            pltpu.SemaphoreType.DMA((6, 4 + links)),
            pltpu.SemaphoreType.DMA((6, 4 + links)),
        ],
        compiler_params=pltpu.CompilerParams(
            collective_id=0, has_side_effects=True, vmem_limit_bytes=60 * 1024 * 1024
        ),
    )(features, targets, mappable[None, :], w_in, w_conv, w_out, w_head)
    grad_in, grad_conv, grad_out = pl.pallas_call(
        functools.partial(deliver, n),
        out_shape=(
            jax.ShapeDtypeStruct((2, channels // n, hid), F32),
            jax.ShapeDtypeStruct((3, hid // n, 2, hid), F32),
            jax.ShapeDtypeStruct((hid // n, 2, channels), F32),
        ),
        in_specs=[vmem],
        out_specs=(vmem, vmem, vmem),
    )(result)
    return (grad_in, jnp.transpose(grad_conv, (2, 0, 1, 3)), jnp.transpose(grad_out, (1, 0, 2)))


def solution(mesh):
    in_specs = (
        P(("grp", "seq"), None),
        P(("grp", "seq"), None),
        P(("grp", "seq")),
        P(),
        P(),
        P(),
        P(),
    )
    out_specs = (P("grp", "seq", None), P("grp", None, "seq", None), P("grp", "seq", None))
    return jax.shard_map(local, mesh=mesh, in_specs=in_specs, out_specs=out_specs, check_vma=False)
```

```python
import functools
import math

import jax
import jax.numpy as jnp
from jax import lax
from jax.experimental import pallas as pl
from jax.experimental.pallas import tpu as pltpu
from jax.sharding import PartitionSpec as P

FIRST_DILATION = 2048
SECOND_DILATION = 4096

TANH_COEF = 0.7978845608028654
CUBIC_COEF = 0.044715
LANES = 128
CHUNK = 32
Z_FIRST = ((1, 0), (1, 2), )
BF16 = jnp.bfloat16
F32 = jnp.float32


def dot(left, right):
    return jnp.dot(left, right, preferred_element_type=F32)


def dot_t(left, right):
    return lax.dot_general(left, right, (((1,), (1,)), ((), ())), preferred_element_type=F32)


def grad_dot(left, right):
    return lax.dot_general(left, right, (((0,), (0,)), ((), ())), preferred_element_type=F32)


def plan(n, hid, channels):
    per_chip = 2 * hid // n
    out = [("out", j, per_chip) for j in range(channels // LANES)]
    conv = [("conv%d" % t, j, per_chip) for t in range(3) for j in range(hid // LANES)]
    inner = [("in", j, 2 * channels // n) for j in range(hid // LANES)]
    segments, start, ends = [], 0, []
    for group in (out, conv, inner):
        for name, column, height in group:
            segments.append((name, column, height, start))
            start += height
        ends.append(start // 32 * 32)
    ends[-1] = -(-start // 32) * 32
    return segments, list(zip([0] + ends[:-1], ends))


def kernel(n, *refs):
    (features, targets_hbm, mappable_hbm, w_in_hbm, w_conv_hbm, w_out_hbm, w_head_hbm, result) = refs[:8]
    (w_in, w_conv, w_out, w_head, stream, counts_out, counts_in, masks) = refs[8:16]
    (hidden, slope_h, middle, slope_m, cot, grad_v, narrow, wide, joined, logit_grad) = refs[16:26]
    (targets, mappable) = refs[26:28]
    (weight_sem, a_send, a_recv, g_send, g_recv) = refs[28:33]
    chunk_refs = {
        (layer, chunk): refs[33 + 8 * (3 * layer + chunk) : 41 + 8 * (3 * layer + chunk)]
        for layer in range(2)
        for chunk in range(3)
    }
    rows, channels = features.shape
    hid = w_in.shape[2]
    tracks = w_head.shape[1]
    links = rows * n // FIRST_DILATION
    part = rows // links
    stride = n // links
    me = lax.axis_index("seq")
    high = me // stride
    low = me % stride
    core = low % 2
    bit_x = (low // 2) % 2
    bit_y = low // 4
    first = bit_x * (1 - core) + bit_y * core
    second = bit_y * (1 - core) + bit_x * core
    sibling = me + 1 - 2 * core
    peer_first = me + (1 - 2 * first) * (2 + 2 * core)
    peer_second = me + (1 - 2 * second) * (4 - 2 * core)

    def chain_peer(k):
        return lax.rem(high + k, links) * stride + low

    def remote(src, dst, send, recv, peer):
        return pltpu.make_async_remote_copy(
            src_ref=src,
            dst_ref=dst,
            send_sem=send,
            recv_sem=recv,
            device_id={"seq": peer},
            device_id_type=pl.DeviceIdType.MESH,
        )

    weight_copies = [
        pltpu.make_async_copy(src, dst, weight_sem.at[i])
        for i, (src, dst) in enumerate(
            ((mappable_hbm, mappable), (targets_hbm, targets), (w_head_hbm, w_head), (w_in_hbm, w_in), (w_conv_hbm, w_conv), (w_out_hbm, w_out))
        )
    ]
    for copy in weight_copies:
        copy.start()

    barrier = pltpu.get_barrier_semaphore()
    partners = [sibling, peer_first, peer_second] + [chain_peer(k) for k in range(1, links)]
    for peer in partners:
        pl.semaphore_signal(
            barrier, inc=1, device_id={"seq": peer}, device_id_type=pl.DeviceIdType.MESH
        )

    def chunks(count, body):
        def step(i, carry):
            body(pl.ds(pl.multiple_of(i * CHUNK, CHUNK), CHUNK))
            return carry

        lax.fori_loop(0, count // CHUNK, step, 0, unroll=True)

    loss_scale = 1.0 / math.sqrt(rows * n)
    def mask_of(p, first_row, count):
        lane = lax.broadcasted_iota(jnp.int32, (count, rows), 1)
        row = lax.broadcasted_iota(jnp.int32, (count, rows), 0)
        values = jnp.broadcast_to(masks[p, :1, :], (count, rows))
        return jnp.sum(jnp.where(lane == row + first_row, values, 0.0), axis=1, keepdims=True)

    pl.semaphore_wait(barrier, len(partners))

    own = pl.ds(pl.multiple_of(high * part, part), part)
    regroup = [[], [], []]

    def send_parts(which, src, dst):
        for k in range(1, links):
            there = pl.ds(pl.multiple_of(lax.rem(high + k, links) * part, part), part)
            copy = remote(
                src.at[there], dst.at[own], a_send.at[which, k], a_recv.at[which, k], chain_peer(k)
            )
            copy.start()
            regroup[which].append(copy)

    send_parts(0, features, stream.at[0])
    own_copy = pltpu.make_async_copy(features.at[own], stream.at[0, own], weight_sem.at[6])
    own_copy.start()
    weight_copies[0].wait()
    masks[high] = jnp.broadcast_to(mappable[...].astype(F32), masks.shape[1:])
    for k in range(1, links):
        copy = remote(masks.at[high], masks.at[high], a_send.at[2, k], a_recv.at[2, k], chain_peer(k))
        copy.start()
        regroup[2].append(copy)
    weight_copies[1].wait()
    logit_grad[...] = (targets[...].astype(F32) * mask_of(high, 0, rows)).astype(BF16)
    weight_copies[2].wait()
    counts_out[...] = (dot_t(logit_grad[...], w_head[...]) * (0.5 * loss_scale)).astype(BF16)
    counts_in[own, :] = counts_out[own, :]
    for copy in regroup[0]:
        copy.wait_send()
    send_parts(1, counts_out, counts_in)

    def swap(value):
        half = value.shape[1] // 2
        return jnp.concatenate([value[:, half:], value[:, :half]], axis=1)

    def mirror(p):
        return rows + (links - 1 - p) * part

    def chain_chunks(body):
        for p in range(links):

            def step(i, carry, p=p):
                offset = pl.multiple_of(i * CHUNK, CHUNK)
                body(pl.ds(p * part + offset, CHUNK), pl.ds(mirror(p) + offset, CHUNK))
                return carry

            lax.fori_loop(0, part // CHUNK, step, 0, unroll=True)

    def activate(value_ref, slope_ref, layer):
        def body(at):
            v = narrow[at, :]
            square = v * v
            tangent = jnp.tanh(TANH_COEF * (v + CUBIC_COEF * square * v))
            value_ref[layer, at, :] = (0.5 * v * (1.0 + tangent)).astype(BF16)
            slope_ref[layer, at, :] = 0.5 * (1.0 + tangent) + 0.5 * v * (
                1.0 - tangent * tangent
            ) * TANH_COEF * (1.0 + 3.0 * CUBIC_COEF * square)

        chunks(2 * rows, body)

    def strand(s):
        return slice(s * rows, (s + 1) * rows)

    def ends(s, skip):
        return slice(s * rows + skip, (s + 1) * rows), slice(s * rows, (s + 1) * rows - skip)

    steps_of = (1, SECOND_DILATION // FIRST_DILATION)

    own_copy.wait()
    for copy in regroup[0]:
        copy.wait_recv()

    def spread(at, across):
        stream[0, across, :] = swap(stream[0, at, :])

    chain_chunks(spread)
    for copy in weight_copies[3:]:
        copy.wait()

    for layer in range(2):
        skip = steps_of[layer] * part
        for s in range(2):
            narrow[strand(s), :] = dot(stream[layer, strand(s), :], w_in[layer])
        activate(hidden, slope_h, layer)
        for s in range(2):
            narrow[strand(s), :] = dot(hidden[layer, strand(s), :], w_conv[layer, 1])
            after, before = ends(s, skip)
            narrow[after, :] += dot(hidden[layer, before, :], w_conv[layer, 0])
            narrow[before, :] += dot(hidden[layer, after, :], w_conv[layer, 2])
        activate(middle, slope_m, layer)
        for s in range(2):
            wide[strand(s), :] = dot(middle[layer, strand(s), :], w_out[layer])

        def add(at, layer=layer):
            stream[layer + 1, at, :] = (stream[layer, at, :].astype(F32) + wide[at, :]).astype(BF16)

        chunks(2 * rows, add)

    def join(at, across):
        joined[at, :] = (
            0.5 * (stream[2, at, :].astype(F32) + swap(stream[2, across, :]).astype(F32))
        ).astype(BF16)

    chain_chunks(join)
    for copy in regroup[2]:
        copy.wait()
    mask = jnp.concatenate([mask_of(p, high * part, part) for p in range(links)], axis=0) * loss_scale
    for panel in range(tracks // LANES):
        at_panel = slice(panel * LANES, (panel + 1) * LANES)
        logits = dot(joined[...], w_head[:, at_panel])
        logit_grad[:, at_panel] = (mask * jnp.exp(logits)).astype(BF16)
    wide[:rows, :] = dot_t(logit_grad[...], w_head[...])
    for copy in regroup[1]:
        copy.wait()

    def divide(at, across):
        incoming = (0.5 * wide[at, :] - counts_in[at, :].astype(F32)).astype(BF16)
        cot[at, :] = incoming
        cot[across, :] = swap(incoming)

    chain_chunks(divide)

    quads = [(h, y, x) for h in range(links) for y in range(2) for x in range(2)]
    segments, chunk_ends = plan(n, hid, channels)
    values = [{}, {}]

    def place(layer, chunk):
        begin, end = chunk_ends[chunk]
        half_rows = (end - begin) // 2
        for half in range(2):
            low_row, high_row = begin + half * half_rows, begin + (half + 1) * half_rows
            for j, (h, y, x) in enumerate(quads):
                b, a = (y, x) if half == 0 else (x, y)
                pieces, filled = [], 0
                for name, column, height, start in segments:
                    first_row, last_row = max(start, low_row), min(start + height, high_row)
                    if first_row >= last_row:
                        continue
                    base = j * height - start
                    at_column = slice(column * LANES, (column + 1) * LANES)
                    pieces.append(
                        values[layer][name][base + first_row : base + last_row, at_column]
                    )
                    filled += last_row - first_row
                if filled < half_rows:
                    pieces.append(jnp.zeros((half_rows - filled, LANES), F32))
                block = pieces[0] if len(pieces) == 1 else jnp.concatenate(pieces, axis=0)
                chunk_refs[layer, chunk][0][half, h, b, a] = block.astype(BF16)

    class Scatter:
        def __init__(self, layer, chunk):
            (self.sums, recv0, *pairs) = chunk_refs[layer, chunk]
            self.send, self.recv = [None] + pairs[0::2], [recv0] + pairs[1::2]
            self.layer, self.index = layer, 3 * layer + chunk
            begin, end = chunk_ends[chunk]
            half = (end - begin) // 2
            self.own = pl.ds(pl.multiple_of(begin + core * half, 16), half)
            self.stage, self.copies = 0, []

        def start(self, src, dst, sem, peer):
            copy = remote(src, dst, g_send.at[self.index, sem], g_recv.at[self.index, sem], peer)
            copy.start()
            self.copies.append(copy)

        def finish(self):
            for copy in self.copies:
                copy.wait()
            self.copies = []

        def advance(self):
            self.finish()
            (self.to_sibling, *self.stages(), self.to_result)[self.stage]()
            self.stage += 1

        def to_sibling(self):
            self.start(self.sums.at[1 - core], self.recv[0], 0, sibling)

        def pair(self, h, b, a):
            return self.sums[core, h, b, a].astype(F32) + self.recv[0][h, b, a].astype(F32)

        def to_result(self):
            result[self.layer, self.own, :] = self.total()
            here = result.at[self.layer, self.own]
            self.start(here, here, 3, sibling)

        def along_chain(self, stage, value):
            for k in range(1, links):
                self.send[stage][k] = value(lax.rem(high + k, links)).astype(BF16)
                self.start(
                    self.send[stage].at[k], self.recv[stage].at[k], 3 + k, chain_peer(k)
                )

        def from_chain(self, stage, total):
            for k in range(1, links):
                total = total + self.recv[stage][k].astype(F32)
            return total

    class PlaneFirst(Scatter):
        def stages(self):
            return self.to_first, self.to_second, self.to_chain

        def after_first(self, h, b):
            return self.pair(h, b, first) + self.recv[1][h, b].astype(F32)

        def after_second(self, h):
            return self.after_first(h, second) + self.recv[2][h].astype(F32)

        def to_first(self):
            for h in range(links):
                for b in range(2):
                    self.send[1][h, b] = self.pair(h, b, 1 - first).astype(BF16)
            self.start(self.send[1], self.recv[1], 1, peer_first)

        def to_second(self):
            for h in range(links):
                self.send[2][h] = self.after_first(h, 1 - second).astype(BF16)
            self.start(self.send[2], self.recv[2], 2, peer_second)

        def to_chain(self):
            self.along_chain(3, self.after_second)

        def total(self):
            return self.from_chain(3, self.after_second(high))

    class ChainFirst(Scatter):
        def stages(self):
            return self.to_chain, self.to_first, self.to_second

        def to_chain(self):
            def value(h):
                return jnp.stack([jnp.stack([self.pair(h, b, a) for a in range(2)]) for b in range(2)])

            self.along_chain(1, value)

        def after_chain(self, b, a):
            total = self.pair(high, b, a)
            for k in range(1, links):
                total = total + self.recv[1][k, b, a].astype(F32)
            return total

        def after_first(self, b):
            return self.after_chain(b, first) + self.recv[2][b].astype(F32)

        def to_first(self):
            for b in range(2):
                self.send[2][b] = self.after_chain(b, 1 - first).astype(BF16)
            self.start(self.send[2], self.recv[2], 1, peer_first)

        def to_second(self):
            self.send[3][...] = self.after_first(1 - second).astype(BF16)
            self.start(self.send[3], self.recv[3], 2, peer_second)

        def total(self):
            return self.after_first(second) + self.recv[3][...].astype(F32)

    scatters = {
        name: (ChainFirst if name in Z_FIRST else PlaneFirst)(*name) for name in chunk_refs
    }

    def advance(*which):
        for name in which:
            scatters[name].advance()

    def grads_out(layer):
        values[layer]["out"] = grad_dot(middle[layer], cot[...])
        place(layer, 0)

    def slopes_mid(layer):
        for s in range(2):
            narrow[strand(s), :] = dot_t(cot[strand(s), :], w_out[layer])

        def slope(at):
            grad_v[at, :] = (narrow[at, :] * slope_m[layer, at, :]).astype(BF16)

        chunks(2 * rows, slope)

    def grads_conv(layer):
        spans = [ends(s, steps_of[layer] * part) for s in range(2)]

        def joined_rows(read, side):
            return jnp.concatenate([read(spans[s][side]) for s in range(2)], axis=0)

        def read_hidden(at):
            return hidden[layer, at, :]

        def read_grad(at):
            return grad_v[at, :]

        values[layer]["conv0"] = grad_dot(joined_rows(read_hidden, 1), joined_rows(read_grad, 0))
        values[layer]["conv1"] = grad_dot(hidden[layer], grad_v[...])
        values[layer]["conv2"] = grad_dot(joined_rows(read_hidden, 0), joined_rows(read_grad, 1))
        place(layer, 1)

    def slopes_in(layer):
        for s in range(2):
            narrow[strand(s), :] = dot_t(grad_v[strand(s), :], w_conv[layer, 1])
            after, before = ends(s, steps_of[layer] * part)
            narrow[before, :] += dot_t(grad_v[after, :], w_conv[layer, 0])
            narrow[after, :] += dot_t(grad_v[before, :], w_conv[layer, 2])

        def slope_back(at):
            grad_v[at, :] = (narrow[at, :] * slope_h[layer, at, :]).astype(BF16)

        chunks(2 * rows, slope_back)

    def grads_in(layer):
        values[layer]["in"] = grad_dot(stream[layer], grad_v[...])
        place(layer, 2)

    def renew_cot():
        for s in range(2):
            wide[strand(s), :] = dot_t(grad_v[strand(s), :], w_in[1])

        def renew(at):
            cot[at, :] = (cot[at, :].astype(F32) + wide[at, :]).astype(BF16)

        chunks(2 * rows, renew)

    grads_out(1)
    advance((1, 0))
    slopes_mid(1)
    grads_conv(1)
    advance((1, 1), (1, 0))
    slopes_in(1)
    grads_in(1)
    renew_cot()
    advance((1, 1))
    grads_out(0)
    advance((0, 0), (1, 2))
    slopes_mid(0)
    grads_conv(0)
    advance((0, 1), (0, 0))
    slopes_in(0)
    advance((1, 2))
    grads_in(0)
    advance((0, 1), (0, 2), (1, 1), (0, 2), (0, 0), (0, 1), (1, 1), (0, 2))
    advance((1, 0), (0, 0), (0, 1), (1, 2), (0, 2), (1, 1), (1, 2), (1, 0))
    advance((1, 0), (0, 1), (0, 0), (1, 2), (0, 2))
    for scatter in scatters.values():
        assert scatter.stage == 5
        scatter.finish()


def deliver(n, result, out_in, out_conv, out_out):
    core = lax.axis_index("seq") % 2
    segments, _ = plan(n, out_conv.shape[3], out_out.shape[2])
    for c in range(2):

        @pl.when(core == c)
        def _(c=c):
            for layer in range(2):
                for name, column, height, start in segments:
                    own = height // 2
                    value = result[layer, start + c * own : start + (c + 1) * own, :]
                    lanes = slice(column * LANES, (column + 1) * LANES)
                    if name == "in":
                        out_in[layer, :, lanes] = value
                    elif name == "out":
                        out_out[:, layer, lanes] = value
                    else:
                        out_conv[int(name[-1]), :, layer, lanes] = value


def local(features, targets, mappable, w_in, w_conv, w_out, w_head):
    rows, channels = features.shape
    n = lax.axis_size("seq")
    links = rows * n // FIRST_DILATION
    hid = w_in.shape[2]
    tracks = targets.shape[1]
    both = 2 * rows
    vmem = pl.BlockSpec(memory_space=pltpu.VMEM)
    hbm = pl.BlockSpec(memory_space=pl.ANY)
    chunk_shapes = []
    _, chunk_ends = plan(n, hid, channels)
    for layer in range(2):
        for chunk, (begin, end) in enumerate(chunk_ends):
            steps = ((links, 2), (links,), (links,))
            if (layer, chunk) in Z_FIRST:
                steps = ((links, 2, 2), (2,), ())
            for lead in ((2, links, 2, 2), (links, 2, 2), *(step for step in steps for _ in range(2))):
                chunk_shapes.append(pltpu.VMEM(lead + ((end - begin) // 2, LANES), BF16))
    result = pl.pallas_call(
        functools.partial(kernel, n),
        out_shape=jax.ShapeDtypeStruct((2, chunk_ends[-1][1], LANES), F32),
        in_specs=[hbm] * 7,
        out_specs=vmem,
        scratch_shapes=[
            pltpu.VMEM(w_in.shape, BF16),
            pltpu.VMEM(w_conv.shape, BF16),
            pltpu.VMEM(w_out.shape, BF16),
            pltpu.VMEM(w_head.shape, BF16),
            pltpu.VMEM((3, both, channels), BF16),
            pltpu.VMEM((rows, channels), BF16),
            pltpu.VMEM((rows, channels), BF16),
            pltpu.VMEM((links, 8, rows), F32),
            pltpu.VMEM((2, both, hid), BF16),
            pltpu.VMEM((2, both, hid), F32),
            pltpu.VMEM((2, both, hid), BF16),
            pltpu.VMEM((2, both, hid), F32),
            pltpu.VMEM((both, channels), BF16),
            pltpu.VMEM((both, hid), BF16),
            pltpu.VMEM((both, hid), F32),
            pltpu.VMEM((both, channels), F32),
            pltpu.VMEM((rows, channels), BF16),
            pltpu.VMEM((rows, tracks), BF16),
            pltpu.VMEM((rows, tracks), jnp.int32),
            pltpu.VMEM((1, rows), jnp.int32),
            pltpu.SemaphoreType.DMA((7,)),
            pltpu.SemaphoreType.DMA((3, links)),
            pltpu.SemaphoreType.DMA((3, links)),
            pltpu.SemaphoreType.DMA((6, 3 + links)),
            pltpu.SemaphoreType.DMA((6, 3 + links)),
            *chunk_shapes,
        ],
        compiler_params=pltpu.CompilerParams(
            collective_id=0, has_side_effects=True, vmem_limit_bytes=60 * 1024 * 1024
        ),
    )(features, targets, mappable[None, :], w_in, w_conv, w_out, w_head)
    grad_in, grad_conv, grad_out = pl.pallas_call(
        functools.partial(deliver, n),
        out_shape=(
            jax.ShapeDtypeStruct((2, channels // n, hid), F32),
            jax.ShapeDtypeStruct((3, hid // n, 2, hid), F32),
            jax.ShapeDtypeStruct((hid // n, 2, channels), F32),
        ),
        in_specs=[vmem],
        out_specs=(vmem, vmem, vmem),
    )(result)
    return (grad_in, jnp.transpose(grad_conv, (2, 0, 1, 3)), jnp.transpose(grad_out, (1, 0, 2)))


def solution(mesh):
    in_specs = (
        P(("grp", "seq"), None),
        P(("grp", "seq"), None),
        P(("grp", "seq")),
        P(),
        P(),
        P(),
        P(),
    )
    out_specs = (P("grp", "seq", None), P("grp", None, "seq", None), P("grp", "seq", None))
    return jax.shard_map(local, mesh=mesh, in_specs=in_specs, out_specs=out_specs, check_vma=False)
```

```python
import functools
import math

import jax
import jax.numpy as jnp
from jax import lax
from jax.experimental import pallas as pl
from jax.experimental.pallas import tpu as pltpu
from jax.sharding import PartitionSpec as P

FIRST_DILATION = 2048
SECOND_DILATION = 4096

TANH_COEF = 0.7978845608028654
CUBIC_COEF = 0.044715
LANES = 128
CHUNK = 32
Z_FIRST = ((1, 0), (1, 2), )
BF16 = jnp.bfloat16
F32 = jnp.float32


def dot(left, right):
    return jnp.dot(left, right, preferred_element_type=F32)


def dot_t(left, right):
    return lax.dot_general(left, right, (((1,), (1,)), ((), ())), preferred_element_type=F32)


def grad_dot(left, right):
    return lax.dot_general(left, right, (((0,), (0,)), ((), ())), preferred_element_type=F32)


def plan(n, hid, channels):
    per_chip = 2 * hid // n
    out = [("out", j, per_chip) for j in range(channels // LANES)]
    conv = [("conv%d" % t, j, per_chip) for t in range(3) for j in range(hid // LANES)]
    inner = [("in", j, 2 * channels // n) for j in range(hid // LANES)]
    segments, start, ends = [], 0, []
    for group in (out, conv, inner):
        for name, column, height in group:
            segments.append((name, column, height, start))
            start += height
        ends.append(start // 32 * 32)
    ends[-1] = -(-start // 32) * 32
    return segments, list(zip([0] + ends[:-1], ends))


def kernel(n, *refs):
    (features, targets_hbm, mappable_hbm, w_in_hbm, w_conv_hbm, w_out_hbm, w_head_hbm, result) = refs[:8]
    (w_in, w_conv, w_out, w_head, stream, counts_out, counts_in, masks) = refs[8:16]
    (hidden, slope_h, middle, slope_m, cot, grad_m, narrow, wide, joined, logit_grad) = refs[16:26]
    (targets, mappable, grad_h) = refs[26:29]
    (weight_sem, a_send, a_recv, g_send, g_recv) = refs[29:34]
    chunk_refs = {
        (layer, chunk): refs[34 + 8 * (3 * layer + chunk) : 42 + 8 * (3 * layer + chunk)]
        for layer in range(2)
        for chunk in range(3)
    }
    rows, channels = features.shape
    hid = w_in.shape[2]
    tracks = w_head.shape[1]
    links = rows * n // FIRST_DILATION
    part = rows // links
    stride = n // links
    me = lax.axis_index("seq")
    high = me // stride
    low = me % stride
    core = low % 2
    bit_x = (low // 2) % 2
    bit_y = low // 4
    first = bit_x * (1 - core) + bit_y * core
    second = bit_y * (1 - core) + bit_x * core
    sibling = me + 1 - 2 * core
    peer_first = me + (1 - 2 * first) * (2 + 2 * core)
    peer_second = me + (1 - 2 * second) * (4 - 2 * core)

    upper = high // (links // 2)

    def chain_peer(k):
        return lax.rem(high + k, links) * stride + low

    def remote(src, dst, send, recv, peer):
        return pltpu.make_async_remote_copy(
            src_ref=src,
            dst_ref=dst,
            send_sem=send,
            recv_sem=recv,
            device_id={"seq": peer},
            device_id_type=pl.DeviceIdType.MESH,
        )

    barrier = pltpu.get_barrier_semaphore()
    partners = [sibling, peer_first, peer_second] + [chain_peer(k) for k in range(1, links)]
    for peer in partners:
        pl.semaphore_signal(
            barrier, inc=1, device_id={"seq": peer}, device_id_type=pl.DeviceIdType.MESH
        )

    weight_copies = [
        pltpu.make_async_copy(src, dst, weight_sem.at[i])
        for i, (src, dst) in enumerate(
            ((mappable_hbm, mappable), (targets_hbm, targets), (w_head_hbm, w_head), (w_in_hbm, w_in), (w_conv_hbm, w_conv), (w_out_hbm, w_out))
        )
    ]
    for copy in weight_copies:
        copy.start()

    def chunks(count, body):
        def step(i, carry):
            body(pl.ds(pl.multiple_of(i * CHUNK, CHUNK), CHUNK))
            return carry

        lax.fori_loop(0, count // CHUNK, step, 0, unroll=True)

    loss_scale = 1.0 / math.sqrt(rows * n)
    def mask_of(p, first_row, count):
        lane = lax.broadcasted_iota(jnp.int32, (count, rows), 1)
        row = lax.broadcasted_iota(jnp.int32, (count, rows), 0)
        values = jnp.broadcast_to(masks[p, :1, :], (count, rows))
        return jnp.sum(jnp.where(lane == row + first_row, values, 0.0), axis=1, keepdims=True)

    pl.semaphore_wait(barrier, len(partners))

    own = pl.ds(pl.multiple_of(high * part, part), part)
    regroup = [[], [], []]

    def send_parts(which, src, dst):
        for turn in range(1, links):
            k = upper * turn + (1 - upper) * (links - turn)
            there = pl.ds(pl.multiple_of(lax.rem(high + k, links) * part, part), part)
            copy = remote(
                src.at[there], dst.at[own], a_send.at[which, k], a_recv.at[which, k], chain_peer(k)
            )
            copy.start()
            regroup[which].append(copy)

    send_parts(0, features, stream.at[0])
    own_copy = pltpu.make_async_copy(features.at[own], stream.at[0, own], weight_sem.at[6])
    own_copy.start()
    weight_copies[0].wait()
    masks[high] = jnp.broadcast_to(mappable[...].astype(F32), masks.shape[1:])
    for k in range(1, links):
        copy = remote(masks.at[high], masks.at[high], a_send.at[2, k], a_recv.at[2, k], chain_peer(k))
        copy.start()
        regroup[2].append(copy)
    weight_copies[1].wait()
    logit_grad[...] = (targets[...].astype(F32) * mask_of(high, 0, rows)).astype(BF16)
    weight_copies[2].wait()
    counts_out[...] = (dot_t(logit_grad[...], w_head[...]) * (0.5 * loss_scale)).astype(BF16)
    counts_in[own, :] = counts_out[own, :]
    for copy in regroup[0]:
        copy.wait_send()
    send_parts(1, counts_out, counts_in)

    def swap(value):
        half = value.shape[1] // 2
        return jnp.concatenate([value[:, half:], value[:, :half]], axis=1)

    def mirror(p):
        return rows + (links - 1 - p) * part

    def chain_chunks(body):
        for p in range(links):

            def step(i, carry, p=p):
                offset = pl.multiple_of(i * CHUNK, CHUNK)
                body(pl.ds(p * part + offset, CHUNK), pl.ds(mirror(p) + offset, CHUNK))
                return carry

            lax.fori_loop(0, part // CHUNK, step, 0, unroll=True)

    def activate(value_ref, slope_ref, layer):
        def body(at):
            v = narrow[at, :]
            square = v * v
            tangent = jnp.tanh(TANH_COEF * (v + CUBIC_COEF * square * v))
            value_ref[layer, at, :] = (0.5 * v * (1.0 + tangent)).astype(BF16)
            slope_ref[layer, at, :] = 0.5 * (1.0 + tangent) + 0.5 * v * (
                1.0 - tangent * tangent
            ) * TANH_COEF * (1.0 + 3.0 * CUBIC_COEF * square)

        chunks(2 * rows, body)

    def strand(s):
        return slice(s * rows, (s + 1) * rows)

    def ends(s, skip):
        return slice(s * rows + skip, (s + 1) * rows), slice(s * rows, (s + 1) * rows - skip)

    steps_of = (1, SECOND_DILATION // FIRST_DILATION)

    own_copy.wait()
    for copy in regroup[0]:
        copy.wait_recv()

    def spread(at, across):
        stream[0, across, :] = swap(stream[0, at, :])

    chain_chunks(spread)
    for copy in weight_copies[3:]:
        copy.wait()

    for layer in range(2):
        skip = steps_of[layer] * part
        for s in range(2):
            narrow[strand(s), :] = dot(stream[layer, strand(s), :], w_in[layer])
        activate(hidden, slope_h, layer)
        for s in range(2):
            narrow[strand(s), :] = dot(hidden[layer, strand(s), :], w_conv[layer, 1])
            after, before = ends(s, skip)
            narrow[after, :] += dot(hidden[layer, before, :], w_conv[layer, 0])
            narrow[before, :] += dot(hidden[layer, after, :], w_conv[layer, 2])
        activate(middle, slope_m, layer)
        for s in range(2):
            wide[strand(s), :] = dot(middle[layer, strand(s), :], w_out[layer])

        def add(at, layer=layer):
            stream[layer + 1, at, :] = (stream[layer, at, :].astype(F32) + wide[at, :]).astype(BF16)

        chunks(2 * rows, add)

    def join(at, across):
        joined[at, :] = (
            0.5 * (stream[2, at, :].astype(F32) + swap(stream[2, across, :]).astype(F32))
        ).astype(BF16)

    chain_chunks(join)
    for copy in regroup[2]:
        copy.wait()
    mask = jnp.concatenate([mask_of(p, high * part, part) for p in range(links)], axis=0) * loss_scale
    for panel in range(tracks // LANES):
        at_panel = slice(panel * LANES, (panel + 1) * LANES)
        logits = dot(joined[...], w_head[:, at_panel])
        logit_grad[:, at_panel] = (mask * jnp.exp(logits)).astype(BF16)
    wide[:rows, :] = dot_t(logit_grad[...], w_head[...])
    for copy in regroup[1]:
        copy.wait()

    def divide(at, across):
        incoming = (0.5 * wide[at, :] - counts_in[at, :].astype(F32)).astype(BF16)
        cot[1, at, :] = incoming
        cot[1, across, :] = swap(incoming)

    chain_chunks(divide)

    quads = [(h, y, x) for h in range(links) for y in range(2) for x in range(2)]
    segments, chunk_ends = plan(n, hid, channels)
    values = [{}, {}]

    def place(layer, chunk):
        begin, end = chunk_ends[chunk]
        half_rows = (end - begin) // 2
        for half in range(2):
            low_row, high_row = begin + half * half_rows, begin + (half + 1) * half_rows
            for j, (h, y, x) in enumerate(quads):
                b, a = (y, x) if half == 0 else (x, y)
                pieces, filled = [], 0
                for name, column, height, start in segments:
                    first_row, last_row = max(start, low_row), min(start + height, high_row)
                    if first_row >= last_row:
                        continue
                    base = j * height - start
                    at_column = slice(column * LANES, (column + 1) * LANES)
                    pieces.append(
                        values[layer][name][base + first_row : base + last_row, at_column]
                    )
                    filled += last_row - first_row
                if filled < half_rows:
                    pieces.append(jnp.zeros((half_rows - filled, LANES), F32))
                block = pieces[0] if len(pieces) == 1 else jnp.concatenate(pieces, axis=0)
                chunk_refs[layer, chunk][0][half, h, b, a] = block.astype(BF16)

    class Scatter:
        def __init__(self, layer, chunk):
            (self.sums, recv0, *pairs) = chunk_refs[layer, chunk]
            self.send, self.recv = [None] + pairs[0::2], [recv0] + pairs[1::2]
            self.layer, self.index = layer, 3 * layer + chunk
            begin, end = chunk_ends[chunk]
            half = (end - begin) // 2
            self.own = pl.ds(pl.multiple_of(begin + core * half, 16), half)
            self.stage, self.copies = 0, []

        def start(self, src, dst, sem, peer):
            copy = remote(src, dst, g_send.at[self.index, sem], g_recv.at[self.index, sem], peer)
            copy.start()
            self.copies.append(copy)

        def finish(self):
            for copy in self.copies:
                copy.wait()
            self.copies = []

        def advance(self):
            self.finish()
            (self.to_sibling, *self.stages(), self.to_result)[self.stage]()
            self.stage += 1

        def to_sibling(self):
            self.start(self.sums.at[1 - core], self.recv[0], 0, sibling)

        def pair(self, h, b, a):
            return self.sums[core, h, b, a].astype(F32) + self.recv[0][h, b, a].astype(F32)

        def to_result(self):
            result[self.layer, self.own, :] = self.total()
            here = result.at[self.layer, self.own]
            self.start(here, here, 3, sibling)

        def along_chain(self, stage, value):
            for turn in range(1, links):
                k = upper * turn + (1 - upper) * (links - turn)
                self.send[stage][k] = value(lax.rem(high + k, links)).astype(BF16)
                self.start(
                    self.send[stage].at[k], self.recv[stage].at[k], 3 + k, chain_peer(k)
                )

        def from_chain(self, stage, total):
            for k in range(1, links):
                total = total + self.recv[stage][k].astype(F32)
            return total

    class PlaneFirst(Scatter):
        def stages(self):
            return self.to_first, self.to_second, self.to_chain

        def after_first(self, h, b):
            return self.pair(h, b, first) + self.recv[1][h, b].astype(F32)

        def after_second(self, h):
            return self.after_first(h, second) + self.recv[2][h].astype(F32)

        def to_first(self):
            for h in range(links):
                for b in range(2):
                    self.send[1][h, b] = self.pair(h, b, 1 - first).astype(BF16)
            self.start(self.send[1], self.recv[1], 1, peer_first)

        def to_second(self):
            for h in range(links):
                self.send[2][h] = self.after_first(h, 1 - second).astype(BF16)
            self.start(self.send[2], self.recv[2], 2, peer_second)

        def to_chain(self):
            self.along_chain(3, self.after_second)

        def total(self):
            return self.from_chain(3, self.after_second(high))

    class ChainFirst(Scatter):
        def stages(self):
            return self.to_chain, self.to_first, self.to_second

        def to_chain(self):
            def value(h):
                return jnp.stack([jnp.stack([self.pair(h, b, a) for a in range(2)]) for b in range(2)])

            self.along_chain(1, value)

        def after_chain(self, b, a):
            total = self.pair(high, b, a)
            for k in range(1, links):
                total = total + self.recv[1][k, b, a].astype(F32)
            return total

        def after_first(self, b):
            return self.after_chain(b, first) + self.recv[2][b].astype(F32)

        def to_first(self):
            for b in range(2):
                self.send[2][b] = self.after_chain(b, 1 - first).astype(BF16)
            self.start(self.send[2], self.recv[2], 1, peer_first)

        def to_second(self):
            self.send[3][...] = self.after_first(1 - second).astype(BF16)
            self.start(self.send[3], self.recv[3], 2, peer_second)

        def total(self):
            return self.after_first(second) + self.recv[3][...].astype(F32)

    scatters = {
        name: (ChainFirst if name in Z_FIRST else PlaneFirst)(*name) for name in chunk_refs
    }

    def advance(*which):
        for name in which:
            scatters[name].advance()

    def grads_out(layer):
        values[layer]["out"] = grad_dot(middle[layer], cot[layer])
        place(layer, 0)

    def slopes_mid(layer):
        for s in range(2):
            narrow[strand(s), :] = dot_t(cot[layer, strand(s), :], w_out[layer])

        def slope(at):
            grad_m[layer, at, :] = (narrow[at, :] * slope_m[layer, at, :]).astype(BF16)

        chunks(2 * rows, slope)

    def grads_conv(layer):
        spans = [ends(s, steps_of[layer] * part) for s in range(2)]

        def joined_rows(read, side):
            return jnp.concatenate([read(spans[s][side]) for s in range(2)], axis=0)

        def read_hidden(at):
            return hidden[layer, at, :]

        def read_grad(at):
            return grad_m[layer, at, :]

        values[layer]["conv0"] = grad_dot(joined_rows(read_hidden, 1), joined_rows(read_grad, 0))
        values[layer]["conv1"] = grad_dot(hidden[layer], grad_m[layer])
        values[layer]["conv2"] = grad_dot(joined_rows(read_hidden, 0), joined_rows(read_grad, 1))
        place(layer, 1)

    def slopes_in(layer):
        for s in range(2):
            narrow[strand(s), :] = dot_t(grad_m[layer, strand(s), :], w_conv[layer, 1])
            after, before = ends(s, steps_of[layer] * part)
            narrow[before, :] += dot_t(grad_m[layer, after, :], w_conv[layer, 0])
            narrow[after, :] += dot_t(grad_m[layer, before, :], w_conv[layer, 2])

        def slope_back(at):
            grad_h[layer, at, :] = (narrow[at, :] * slope_h[layer, at, :]).astype(BF16)

        chunks(2 * rows, slope_back)

    def grads_in(layer):
        values[layer]["in"] = grad_dot(stream[layer], grad_h[layer])
        place(layer, 2)

    def renew_cot():
        for s in range(2):
            wide[strand(s), :] = dot_t(grad_h[1, strand(s), :], w_in[1])

        def renew(at):
            cot[0, at, :] = (cot[1, at, :].astype(F32) + wide[at, :]).astype(BF16)

        chunks(2 * rows, renew)

    grads_out(1)
    advance((1, 0))
    slopes_mid(1)
    grads_conv(1)
    advance((1, 1), (1, 0))
    slopes_in(1)
    grads_in(1)
    advance((1, 2))
    renew_cot()
    advance((1, 1))
    grads_out(0)
    advance((0, 0), (1, 2))
    slopes_mid(0)
    grads_conv(0)
    advance((0, 1), (0, 0))
    slopes_in(0)
    advance((1, 1))
    grads_in(0)
    advance((0, 2), (0, 1), (0, 2), (0, 0), (1, 1), (0, 1), (1, 0), (0, 2))
    advance((0, 0), (1, 2), (0, 1), (1, 0), (0, 2), (1, 1), (1, 2), (1, 0))
    advance((0, 0), (0, 1), (1, 2), (0, 2))
    for scatter in scatters.values():
        assert scatter.stage == 5
        scatter.finish()


def deliver(n, result, out_in, out_conv, out_out):
    core = lax.axis_index("seq") % 2
    segments, _ = plan(n, out_conv.shape[3], out_out.shape[2])
    for c in range(2):

        @pl.when(core == c)
        def _(c=c):
            for layer in range(2):
                for name, column, height, start in segments:
                    own = height // 2
                    value = result[layer, start + c * own : start + (c + 1) * own, :]
                    lanes = slice(column * LANES, (column + 1) * LANES)
                    if name == "in":
                        out_in[layer, :, lanes] = value
                    elif name == "out":
                        out_out[:, layer, lanes] = value
                    else:
                        out_conv[int(name[-1]), :, layer, lanes] = value


def local(features, targets, mappable, w_in, w_conv, w_out, w_head):
    rows, channels = features.shape
    n = lax.axis_size("seq")
    links = rows * n // FIRST_DILATION
    hid = w_in.shape[2]
    tracks = targets.shape[1]
    both = 2 * rows
    vmem = pl.BlockSpec(memory_space=pltpu.VMEM)
    hbm = pl.BlockSpec(memory_space=pl.ANY)
    chunk_shapes = []
    _, chunk_ends = plan(n, hid, channels)
    for layer in range(2):
        for chunk, (begin, end) in enumerate(chunk_ends):
            steps = ((links, 2), (links,), (links,))
            if (layer, chunk) in Z_FIRST:
                steps = ((links, 2, 2), (2,), ())
            for lead in ((2, links, 2, 2), (links, 2, 2), *(step for step in steps for _ in range(2))):
                chunk_shapes.append(pltpu.VMEM(lead + ((end - begin) // 2, LANES), BF16))
    result = pl.pallas_call(
        functools.partial(kernel, n),
        out_shape=jax.ShapeDtypeStruct((2, chunk_ends[-1][1], LANES), F32),
        in_specs=[hbm] * 7,
        out_specs=vmem,
        scratch_shapes=[
            pltpu.VMEM(w_in.shape, BF16),
            pltpu.VMEM(w_conv.shape, BF16),
            pltpu.VMEM(w_out.shape, BF16),
            pltpu.VMEM(w_head.shape, BF16),
            pltpu.VMEM((3, both, channels), BF16),
            pltpu.VMEM((rows, channels), BF16),
            pltpu.VMEM((rows, channels), BF16),
            pltpu.VMEM((links, 8, rows), F32),
            pltpu.VMEM((2, both, hid), BF16),
            pltpu.VMEM((2, both, hid), F32),
            pltpu.VMEM((2, both, hid), BF16),
            pltpu.VMEM((2, both, hid), F32),
            pltpu.VMEM((2, both, channels), BF16),
            pltpu.VMEM((2, both, hid), BF16),
            pltpu.VMEM((both, hid), F32),
            pltpu.VMEM((both, channels), F32),
            pltpu.VMEM((rows, channels), BF16),
            pltpu.VMEM((rows, tracks), BF16),
            pltpu.VMEM((rows, tracks), jnp.int32),
            pltpu.VMEM((1, rows), jnp.int32),
            pltpu.VMEM((2, both, hid), BF16),
            pltpu.SemaphoreType.DMA((7,)),
            pltpu.SemaphoreType.DMA((3, links)),
            pltpu.SemaphoreType.DMA((3, links)),
            pltpu.SemaphoreType.DMA((6, 3 + links)),
            pltpu.SemaphoreType.DMA((6, 3 + links)),
            *chunk_shapes,
        ],
        compiler_params=pltpu.CompilerParams(
            collective_id=0, has_side_effects=True, vmem_limit_bytes=60 * 1024 * 1024
        ),
    )(features, targets, mappable[None, :], w_in, w_conv, w_out, w_head)
    grad_in, grad_conv, grad_out = pl.pallas_call(
        functools.partial(deliver, n),
        out_shape=(
            jax.ShapeDtypeStruct((2, channels // n, hid), F32),
            jax.ShapeDtypeStruct((3, hid // n, 2, hid), F32),
            jax.ShapeDtypeStruct((hid // n, 2, channels), F32),
        ),
        in_specs=[vmem],
        out_specs=(vmem, vmem, vmem),
    )(result)
    return (grad_in, jnp.transpose(grad_conv, (2, 0, 1, 3)), jnp.transpose(grad_out, (1, 0, 2)))


def solution(mesh):
    in_specs = (
        P(("grp", "seq"), None),
        P(("grp", "seq"), None),
        P(("grp", "seq")),
        P(),
        P(),
        P(),
        P(),
    )
    out_specs = (P("grp", "seq", None), P("grp", None, "seq", None), P("grp", "seq", None))
    return jax.shard_map(local, mesh=mesh, in_specs=in_specs, out_specs=out_specs, check_vma=False)
```

```python
import functools
import math

import jax
import jax.numpy as jnp
from jax import lax
from jax.experimental import pallas as pl
from jax.experimental.pallas import tpu as pltpu
from jax.sharding import PartitionSpec as P

FIRST_DILATION = 2048
SECOND_DILATION = 4096

TANH_COEF = 0.7978845608028654
CUBIC_COEF = 0.044715
LANES = 128
CHUNK = 32
Z_FIRST = ((1, 0), (1, 2), )
BF16 = jnp.bfloat16
F32 = jnp.float32


def dot(left, right):
    return jnp.dot(left, right, preferred_element_type=F32)


def dot_t(left, right):
    return lax.dot_general(left, right, (((1,), (1,)), ((), ())), preferred_element_type=F32)


def grad_dot(left, right):
    return lax.dot_general(left, right, (((0,), (0,)), ((), ())), preferred_element_type=F32)


def plan(n, hid, channels):
    per_chip = 2 * hid // n
    out = [("out", j, per_chip) for j in range(channels // LANES)]
    conv = [("conv%d" % t, j, per_chip) for t in range(3) for j in range(hid // LANES)]
    inner = [("in", j, 2 * channels // n) for j in range(hid // LANES)]
    segments, start, ends = [], 0, []
    for group in (out, conv, inner):
        for name, column, height in group:
            segments.append((name, column, height, start))
            start += height
        ends.append(start // 32 * 32)
    ends[-1] = -(-start // 32) * 32
    return segments, list(zip([0] + ends[:-1], ends))


def kernel(n, *refs):
    (features, targets_hbm, mappable_hbm, w_in_hbm, w_conv_hbm, w_out_hbm, w_head_hbm, result) = refs[:8]
    (w_in, w_conv, w_out, w_head, stream, counts_out, counts_in, masks) = refs[8:16]
    (hidden, slope_h, middle, slope_m, cot, grad_m, narrow, wide, joined, logit_grad) = refs[16:26]
    (targets, mappable, grad_h) = refs[26:29]
    (weight_sem, a_send, a_recv, g_send, g_recv) = refs[29:34]
    chunk_refs = {
        (layer, chunk): refs[34 + 8 * (3 * layer + chunk) : 42 + 8 * (3 * layer + chunk)]
        for layer in range(2)
        for chunk in range(3)
    }
    rows, channels = features.shape
    hid = w_in.shape[2]
    tracks = w_head.shape[1]
    links = rows * n // FIRST_DILATION
    part = rows // links
    stride = n // links
    me = lax.axis_index("seq")
    high = me // stride
    low = me % stride
    core = low % 2
    bit_x = (low // 2) % 2
    bit_y = low // 4
    first = bit_x * (1 - core) + bit_y * core
    second = bit_y * (1 - core) + bit_x * core
    sibling = me + 1 - 2 * core
    peer_first = me + (1 - 2 * first) * (2 + 2 * core)
    peer_second = me + (1 - 2 * second) * (4 - 2 * core)

    upper = high // (links // 2)

    def chain_peer(k):
        return lax.rem(high + k, links) * stride + low

    def remote(src, dst, send, recv, peer):
        return pltpu.make_async_remote_copy(
            src_ref=src,
            dst_ref=dst,
            send_sem=send,
            recv_sem=recv,
            device_id={"seq": peer},
            device_id_type=pl.DeviceIdType.MESH,
        )

    barrier = pltpu.get_barrier_semaphore()
    partners = [sibling, peer_first, peer_second] + [chain_peer(k) for k in range(1, links)]
    for peer in partners:
        pl.semaphore_signal(
            barrier, inc=1, device_id={"seq": peer}, device_id_type=pl.DeviceIdType.MESH
        )

    weight_copies = [
        pltpu.make_async_copy(src, dst, weight_sem.at[i])
        for i, (src, dst) in enumerate(
            ((mappable_hbm, mappable), (targets_hbm, targets), (w_head_hbm, w_head), (w_in_hbm, w_in), (w_conv_hbm, w_conv), (w_out_hbm, w_out))
        )
    ]
    for copy in weight_copies:
        copy.start()

    def chunks(count, body):
        def step(i, carry):
            body(pl.ds(pl.multiple_of(i * CHUNK, CHUNK), CHUNK))
            return carry

        lax.fori_loop(0, count // CHUNK, step, 0, unroll=True)

    loss_scale = 1.0 / math.sqrt(rows * n)
    def mask_of(p, first_row, count):
        lane = lax.broadcasted_iota(jnp.int32, (count, rows), 1)
        row = lax.broadcasted_iota(jnp.int32, (count, rows), 0)
        values = jnp.broadcast_to(masks[p, :1, :], (count, rows))
        return jnp.sum(jnp.where(lane == row + first_row, values, 0.0), axis=1, keepdims=True)

    pl.semaphore_wait(barrier, len(partners))

    own = pl.ds(pl.multiple_of(high * part, part), part)
    regroup = [[], [], []]

    def send_parts(which, src, dst):
        for turn in range(1, links):
            k = upper * turn + (1 - upper) * (links - turn)
            there = pl.ds(pl.multiple_of(lax.rem(high + k, links) * part, part), part)
            copy = remote(
                src.at[there], dst.at[own], a_send.at[which, k], a_recv.at[which, k], chain_peer(k)
            )
            copy.start()
            regroup[which].append(copy)

    send_parts(0, features, stream.at[0])
    own_copy = pltpu.make_async_copy(features.at[own], stream.at[0, own], weight_sem.at[6])
    own_copy.start()
    weight_copies[0].wait()
    masks[high] = jnp.broadcast_to(mappable[...].astype(F32), masks.shape[1:])
    for k in range(1, links):
        copy = remote(masks.at[high], masks.at[high], a_send.at[2, k], a_recv.at[2, k], chain_peer(k))
        copy.start()
        regroup[2].append(copy)
    weight_copies[1].wait()
    logit_grad[...] = (targets[...].astype(F32) * mask_of(high, 0, rows)).astype(BF16)
    weight_copies[2].wait()
    counts_out[...] = (dot_t(logit_grad[...], w_head[...]) * (0.5 * loss_scale)).astype(BF16)
    counts_in[own, :] = counts_out[own, :]
    send_parts(1, counts_out, counts_in)

    def swap(value):
        half = value.shape[1] // 2
        return jnp.concatenate([value[:, half:], value[:, :half]], axis=1)

    def mirror(p):
        return rows + (links - 1 - p) * part

    def chain_chunks(body):
        for p in range(links):

            def step(i, carry, p=p):
                offset = pl.multiple_of(i * CHUNK, CHUNK)
                body(pl.ds(p * part + offset, CHUNK), pl.ds(mirror(p) + offset, CHUNK))
                return carry

            lax.fori_loop(0, part // CHUNK, step, 0, unroll=True)

    def activate(value_ref, slope_ref, layer):
        def body(at):
            v = narrow[at, :]
            square = v * v
            tangent = jnp.tanh(TANH_COEF * (v + CUBIC_COEF * square * v))
            value_ref[layer, at, :] = (0.5 * v * (1.0 + tangent)).astype(BF16)
            slope_ref[layer, at, :] = 0.5 * (1.0 + tangent) + 0.5 * v * (
                1.0 - tangent * tangent
            ) * TANH_COEF * (1.0 + 3.0 * CUBIC_COEF * square)

        chunks(2 * rows, body)

    def strand(s):
        return slice(s * rows, (s + 1) * rows)

    def ends(s, skip):
        return slice(s * rows + skip, (s + 1) * rows), slice(s * rows, (s + 1) * rows - skip)

    steps_of = (1, SECOND_DILATION // FIRST_DILATION)

    own_copy.wait()
    for copy in regroup[0]:
        copy.wait()

    def spread(at, across):
        stream[0, across, :] = swap(stream[0, at, :])

    chain_chunks(spread)
    for copy in weight_copies[3:]:
        copy.wait()

    for layer in range(2):
        skip = steps_of[layer] * part
        for s in range(2):
            narrow[strand(s), :] = dot(stream[layer, strand(s), :], w_in[layer])
        activate(hidden, slope_h, layer)
        for s in range(2):
            narrow[strand(s), :] = dot(hidden[layer, strand(s), :], w_conv[layer, 1])
            after, before = ends(s, skip)
            narrow[after, :] += dot(hidden[layer, before, :], w_conv[layer, 0])
            narrow[before, :] += dot(hidden[layer, after, :], w_conv[layer, 2])
        activate(middle, slope_m, layer)
        for s in range(2):
            wide[strand(s), :] = dot(middle[layer, strand(s), :], w_out[layer])

        def add(at, layer=layer):
            stream[layer + 1, at, :] = (stream[layer, at, :].astype(F32) + wide[at, :]).astype(BF16)

        chunks(2 * rows, add)

    def join(at, across):
        joined[at, :] = (
            0.5 * (stream[2, at, :].astype(F32) + swap(stream[2, across, :]).astype(F32))
        ).astype(BF16)

    chain_chunks(join)
    for copy in regroup[2]:
        copy.wait()
    mask = jnp.concatenate([mask_of(p, high * part, part) for p in range(links)], axis=0) * loss_scale
    for panel in range(tracks // LANES):
        at_panel = slice(panel * LANES, (panel + 1) * LANES)
        logits = dot(joined[...], w_head[:, at_panel])
        logit_grad[:, at_panel] = (mask * jnp.exp(logits)).astype(BF16)
    wide[:rows, :] = dot_t(logit_grad[...], w_head[...])
    for copy in regroup[1]:
        copy.wait()

    def divide(at, across):
        incoming = (0.5 * wide[at, :] - counts_in[at, :].astype(F32)).astype(BF16)
        cot[1, at, :] = incoming
        cot[1, across, :] = swap(incoming)

    chain_chunks(divide)

    quads = [(h, y, x) for h in range(links) for y in range(2) for x in range(2)]
    segments, chunk_ends = plan(n, hid, channels)
    values = [{}, {}]

    def place(layer, chunk):
        begin, end = chunk_ends[chunk]
        half_rows = (end - begin) // 2
        for half in range(2):
            low_row, high_row = begin + half * half_rows, begin + (half + 1) * half_rows
            for j, (h, y, x) in enumerate(quads):
                b, a = (y, x) if half == 0 else (x, y)
                pieces, filled = [], 0
                for name, column, height, start in segments:
                    first_row, last_row = max(start, low_row), min(start + height, high_row)
                    if first_row >= last_row:
                        continue
                    base = j * height - start
                    at_column = slice(column * LANES, (column + 1) * LANES)
                    pieces.append(
                        values[layer][name][base + first_row : base + last_row, at_column]
                    )
                    filled += last_row - first_row
                if filled < half_rows:
                    pieces.append(jnp.zeros((half_rows - filled, LANES), F32))
                block = pieces[0] if len(pieces) == 1 else jnp.concatenate(pieces, axis=0)
                chunk_refs[layer, chunk][0][half, h, b, a] = block.astype(BF16)

    class Scatter:
        def __init__(self, layer, chunk):
            (self.sums, recv0, *pairs) = chunk_refs[layer, chunk]
            self.send, self.recv = [None] + pairs[0::2], [recv0] + pairs[1::2]
            self.layer, self.index = layer, 3 * layer + chunk
            begin, end = chunk_ends[chunk]
            half = (end - begin) // 2
            self.own = pl.ds(pl.multiple_of(begin + core * half, 16), half)
            self.stage, self.copies = 0, []

        def start(self, src, dst, sem, peer):
            copy = remote(src, dst, g_send.at[self.index, sem], g_recv.at[self.index, sem], peer)
            copy.start()
            self.copies.append(copy)

        def finish(self):
            for copy in self.copies:
                copy.wait()
            self.copies = []

        def advance(self):
            self.finish()
            (self.to_sibling, *self.stages(), self.to_result)[self.stage]()
            self.stage += 1

        def to_sibling(self):
            self.start(self.sums.at[1 - core], self.recv[0], 0, sibling)

        def pair(self, h, b, a):
            return self.sums[core, h, b, a].astype(F32) + self.recv[0][h, b, a].astype(F32)

        def to_result(self):
            result[self.layer, self.own, :] = self.total()
            here = result.at[self.layer, self.own]
            self.start(here, here, 3, sibling)

        def along_chain(self, stage, value):
            for turn in range(1, links):
                k = upper * turn + (1 - upper) * (links - turn)
                self.send[stage][k] = value(lax.rem(high + k, links)).astype(BF16)
                self.start(
                    self.send[stage].at[k], self.recv[stage].at[k], 3 + k, chain_peer(k)
                )

        def from_chain(self, stage, total):
            for k in range(1, links):
                total = total + self.recv[stage][k].astype(F32)
            return total

    class PlaneFirst(Scatter):
        def stages(self):
            return self.to_first, self.to_second, self.to_chain

        def after_first(self, h, b):
            return self.pair(h, b, first) + self.recv[1][h, b].astype(F32)

        def after_second(self, h):
            return self.after_first(h, second) + self.recv[2][h].astype(F32)

        def to_first(self):
            for h in range(links):
                for b in range(2):
                    self.send[1][h, b] = self.pair(h, b, 1 - first).astype(BF16)
            self.start(self.send[1], self.recv[1], 1, peer_first)

        def to_second(self):
            for h in range(links):
                self.send[2][h] = self.after_first(h, 1 - second).astype(BF16)
            self.start(self.send[2], self.recv[2], 2, peer_second)

        def to_chain(self):
            self.along_chain(3, self.after_second)

        def total(self):
            return self.from_chain(3, self.after_second(high))

    class ChainFirst(Scatter):
        def stages(self):
            return self.to_chain, self.to_first, self.to_second

        def to_chain(self):
            def value(h):
                return jnp.stack([jnp.stack([self.pair(h, b, a) for a in range(2)]) for b in range(2)])

            self.along_chain(1, value)

        def after_chain(self, b, a):
            total = self.pair(high, b, a)
            for k in range(1, links):
                total = total + self.recv[1][k, b, a].astype(F32)
            return total

        def after_first(self, b):
            return self.after_chain(b, first) + self.recv[2][b].astype(F32)

        def to_first(self):
            for b in range(2):
                self.send[2][b] = self.after_chain(b, 1 - first).astype(BF16)
            self.start(self.send[2], self.recv[2], 1, peer_first)

        def to_second(self):
            self.send[3][...] = self.after_first(1 - second).astype(BF16)
            self.start(self.send[3], self.recv[3], 2, peer_second)

        def total(self):
            return self.after_first(second) + self.recv[3][...].astype(F32)

    scatters = {
        name: (ChainFirst if name in Z_FIRST else PlaneFirst)(*name) for name in chunk_refs
    }

    def advance(*which):
        for name in which:
            scatters[name].advance()

    def grads_out(layer):
        values[layer]["out"] = grad_dot(middle[layer], cot[layer])
        place(layer, 0)

    def slopes_mid(layer):
        for s in range(2):
            narrow[strand(s), :] = dot_t(cot[layer, strand(s), :], w_out[layer])

        def slope(at):
            grad_m[layer, at, :] = (narrow[at, :] * slope_m[layer, at, :]).astype(BF16)

        chunks(2 * rows, slope)

    def grads_conv(layer):
        spans = [ends(s, steps_of[layer] * part) for s in range(2)]

        def joined_rows(read, side):
            return jnp.concatenate([read(spans[s][side]) for s in range(2)], axis=0)

        def read_hidden(at):
            return hidden[layer, at, :]

        def read_grad(at):
            return grad_m[layer, at, :]

        values[layer]["conv0"] = grad_dot(joined_rows(read_hidden, 1), joined_rows(read_grad, 0))
        values[layer]["conv1"] = grad_dot(hidden[layer], grad_m[layer])
        values[layer]["conv2"] = grad_dot(joined_rows(read_hidden, 0), joined_rows(read_grad, 1))
        place(layer, 1)

    def slopes_in(layer):
        for s in range(2):
            narrow[strand(s), :] = dot_t(grad_m[layer, strand(s), :], w_conv[layer, 1])
            after, before = ends(s, steps_of[layer] * part)
            narrow[before, :] += dot_t(grad_m[layer, after, :], w_conv[layer, 0])
            narrow[after, :] += dot_t(grad_m[layer, before, :], w_conv[layer, 2])

        def slope_back(at):
            grad_h[layer, at, :] = (narrow[at, :] * slope_h[layer, at, :]).astype(BF16)

        chunks(2 * rows, slope_back)

    def grads_in(layer):
        values[layer]["in"] = grad_dot(stream[layer], grad_h[layer])
        place(layer, 2)

    def renew_cot():
        for s in range(2):
            wide[strand(s), :] = dot_t(grad_h[1, strand(s), :], w_in[1])

        def renew(at):
            cot[0, at, :] = (cot[1, at, :].astype(F32) + wide[at, :]).astype(BF16)

        chunks(2 * rows, renew)

    grads_out(1)
    advance((1, 0))
    slopes_mid(1)
    grads_conv(1)
    advance((1, 1), (1, 0))
    slopes_in(1)
    grads_in(1)
    advance((1, 2))
    renew_cot()
    advance((1, 1))
    grads_out(0)
    advance((0, 0), (1, 2))
    slopes_mid(0)
    grads_conv(0)
    advance((0, 1), (0, 0))
    slopes_in(0)
    advance((1, 1))
    grads_in(0)
    advance((0, 2), (0, 1), (0, 2), (0, 0), (1, 1), (0, 1), (1, 0), (0, 2))
    advance((0, 0), (1, 2), (0, 1), (1, 0), (0, 2), (1, 1), (1, 2), (1, 0))
    advance((0, 0), (0, 1), (1, 2), (0, 2))
    for scatter in scatters.values():
        assert scatter.stage == 5
        scatter.finish()


def deliver(n, result, out_in, out_conv, out_out):
    core = lax.axis_index("seq") % 2
    segments, _ = plan(n, out_conv.shape[3], out_out.shape[2])
    for c in range(2):

        @pl.when(core == c)
        def _(c=c):
            for layer in range(2):
                for name, column, height, start in segments:
                    own = height // 2
                    value = result[layer, start + c * own : start + (c + 1) * own, :]
                    lanes = slice(column * LANES, (column + 1) * LANES)
                    if name == "in":
                        out_in[layer, :, lanes] = value
                    elif name == "out":
                        out_out[:, layer, lanes] = value
                    else:
                        out_conv[int(name[-1]), :, layer, lanes] = value


def local(features, targets, mappable, w_in, w_conv, w_out, w_head):
    rows, channels = features.shape
    n = lax.axis_size("seq")
    links = rows * n // FIRST_DILATION
    hid = w_in.shape[2]
    tracks = targets.shape[1]
    both = 2 * rows
    vmem = pl.BlockSpec(memory_space=pltpu.VMEM)
    hbm = pl.BlockSpec(memory_space=pl.ANY)
    chunk_shapes = []
    _, chunk_ends = plan(n, hid, channels)
    for layer in range(2):
        for chunk, (begin, end) in enumerate(chunk_ends):
            steps = ((links, 2), (links,), (links,))
            if (layer, chunk) in Z_FIRST:
                steps = ((links, 2, 2), (2,), ())
            for lead in ((2, links, 2, 2), (links, 2, 2), *(step for step in steps for _ in range(2))):
                chunk_shapes.append(pltpu.VMEM(lead + ((end - begin) // 2, LANES), BF16))
    result = pl.pallas_call(
        functools.partial(kernel, n),
        out_shape=jax.ShapeDtypeStruct((2, chunk_ends[-1][1], LANES), F32),
        in_specs=[hbm] * 7,
        out_specs=vmem,
        scratch_shapes=[
            pltpu.VMEM(w_in.shape, BF16),
            pltpu.VMEM(w_conv.shape, BF16),
            pltpu.VMEM(w_out.shape, BF16),
            pltpu.VMEM(w_head.shape, BF16),
            pltpu.VMEM((3, both, channels), BF16),
            pltpu.VMEM((rows, channels), BF16),
            pltpu.VMEM((rows, channels), BF16),
            pltpu.VMEM((links, 8, rows), F32),
            pltpu.VMEM((2, both, hid), BF16),
            pltpu.VMEM((2, both, hid), F32),
            pltpu.VMEM((2, both, hid), BF16),
            pltpu.VMEM((2, both, hid), F32),
            pltpu.VMEM((2, both, channels), BF16),
            pltpu.VMEM((2, both, hid), BF16),
            pltpu.VMEM((both, hid), F32),
            pltpu.VMEM((both, channels), F32),
            pltpu.VMEM((rows, channels), BF16),
            pltpu.VMEM((rows, tracks), BF16),
            pltpu.VMEM((rows, tracks), jnp.int32),
            pltpu.VMEM((1, rows), jnp.int32),
            pltpu.VMEM((2, both, hid), BF16),
            pltpu.SemaphoreType.DMA((7,)),
            pltpu.SemaphoreType.DMA((3, links)),
            pltpu.SemaphoreType.DMA((3, links)),
            pltpu.SemaphoreType.DMA((6, 3 + links)),
            pltpu.SemaphoreType.DMA((6, 3 + links)),
            *chunk_shapes,
        ],
        compiler_params=pltpu.CompilerParams(
            collective_id=0, has_side_effects=True, vmem_limit_bytes=60 * 1024 * 1024
        ),
    )(features, targets, mappable[None, :], w_in, w_conv, w_out, w_head)
    grad_in, grad_conv, grad_out = pl.pallas_call(
        functools.partial(deliver, n),
        out_shape=(
            jax.ShapeDtypeStruct((2, channels // n, hid), F32),
            jax.ShapeDtypeStruct((3, hid // n, 2, hid), F32),
            jax.ShapeDtypeStruct((hid // n, 2, channels), F32),
        ),
        in_specs=[vmem],
        out_specs=(vmem, vmem, vmem),
    )(result)
    return (grad_in, jnp.transpose(grad_conv, (2, 0, 1, 3)), jnp.transpose(grad_out, (1, 0, 2)))


def solution(mesh):
    in_specs = (
        P(("grp", "seq"), None),
        P(("grp", "seq"), None),
        P(("grp", "seq")),
        P(),
        P(),
        P(),
        P(),
    )
    out_specs = (P("grp", "seq", None), P("grp", None, "seq", None), P("grp", "seq", None))
    return jax.shard_map(local, mesh=mesh, in_specs=in_specs, out_specs=out_specs, check_vma=False)
```
